128 devices in a mesh: gx: 8 (over y, core), gy: 16 (over z, x).
Axes of the slice: x: 4, y: 4, z: 4, core: 2. Of those that a mesh axis runs over, the one named last changes fastest.
Arguments:
- features: bfloat16 [256, 256, 64, 128], P('gx', 'gy'), may hold values from -6 to 6
- voxel_mask: int32 [256, 256, 64], P('gx', 'gy'), may hold values 0 or 1
- brick_mask: int32 [16, 16, 4], P('gx', 'gy'), may hold values from 0 to 1
- owner: int32 [8, 16, 8, 1], P('gx', 'gy'), may hold values from 0 to 15, as said below
- weights: bfloat16 [3, 3, 3, 128, 64], replicated, may hold values from -0.109375 to 0.109375
- bias: float32 [64], replicated, may hold values from -0.5 to 0.5
Outputs:
- decoded: bfloat16 [8, 256, 64, 4096], P('gx', 'gy')
The draws below stay inside these ranges and needn't reach their ends.
Inputs may be any that keep to these rules, and one draw needn't show every extreme that they name: Active bricks are spread unevenly over tiles. Among one device's 8 bricks no owner index appears more than 1 times, and some index appears exactly 1 times. Owners are chosen from the active-brick counts so that over all sources of one brick-grid row no owner receives more than 8 active bricks.
All inputs are finite; a program needn't handle non-finite values. No bound on the sum of `voxel_mask` on one device may be relied on, other than what follows from the above.
Results may differ from the reference program's by a relative error of at most 0.001.
Values may be sent and summed in bfloat16 or wider, within the bound.
A program may use at most 256 MiB of HBM per device.

```python
import jax
import jax.numpy as jnp
from jax import lax

C = 64
CIN = 128
EDGE = 16
BX = 2
BY = 1
BZ = 4
BRICKS = 8
CAP = 1
NXV = 256
NYV = 256
NZV = 64
N_GX = 8
N_GY = 16


def tile_activity(key):
    tile_key = jax.random.fold_in(key, 11)
    brick_key = jax.random.fold_in(key, 12)
    first = jax.random.randint(jax.random.fold_in(tile_key, 1), (N_GX, N_GY), 0, 9)
    second = jax.random.randint(jax.random.fold_in(tile_key, 2), (N_GX, N_GY), 0, 9)
    level = jnp.minimum(8, 1 + first * second // 8)
    picks = jax.random.randint(brick_key, (N_GX, N_GY, BRICKS), 0, 8)
    return (picks < level[:, :, None]).astype(jnp.int32)


def draw_brick_mask(key, part):
    tile = tile_activity(key)
    grid = tile.reshape(N_GX, N_GY, BX, BY, BZ).transpose(0, 2, 1, 3, 4)
    return grid.reshape(N_GX * BX, N_GY * BY, BZ)


def draw_owner(key, part):
    tile = tile_activity(key)
    active = jnp.sum(tile, axis=2)
    before = jnp.cumsum(active, axis=1) - active
    spare = 1 - tile
    active_rank = jnp.cumsum(tile, axis=2) - tile
    spare_rank = jnp.cumsum(spare, axis=2) - spare
    position = jnp.where(tile == 1, active_rank, active[:, :, None] + spare_rank)
    owners = (before[:, :, None] + position) % N_GY
    return owners[..., None].astype(jnp.int32)


def set_ends(drawn, own_key, least, top_value):
    dims = drawn.shape
    place = [jax.random.randint(jax.random.fold_in(own_key, axis), (), 0, dims[axis]) for axis in range(len(dims))]
    drawn = drawn.at[tuple(place)].set(least)
    longest = dims.index(max(dims))
    place[longest] = (place[longest] + 1) % dims[longest]
    return drawn.at[tuple(place)].set(top_value)


def levels(stream_key, extent, shards, least, top_value):
    def one(dim, blocks):
        heights = jax.random.uniform(jax.random.fold_in(jax.random.fold_in(stream_key, 6), dim), (blocks,), jnp.float32, least / len(shards), top_value / len(shards))
        return jnp.repeat(jnp.exp(heights), extent[dim] // blocks).reshape((-1,) + (1,) * (len(extent) - dim - 1))

    gain = one(*shards[0])
    for cut in shards[1:]:
        gain = gain * one(*cut)
    return gain


def scatter_about(stream_key, shape, scale, most, pieces=(), kind=jnp.bfloat16):
    drawn = scale * jax.random.normal(stream_key, shape, jnp.float32)
    if pieces:
        drawn = drawn * levels(stream_key, shape, pieces, -0.22, 0.18)
    return jnp.clip(drawn, -most, most).astype(kind)


def setup_inputs(seed: int = 0) -> dict:
    keys = jax.random.split(jax.random.key(seed), 7)
    features = scatter_about(keys[0], (NXV, NYV, NZV, CIN), 1.0, 6.0, ((0, 8), (1, 16)))
    voxel_mask = set_ends((jax.random.randint(keys[1], (NXV, NYV, NZV), 0, 3) < 2).astype(jnp.int32), jax.random.fold_in(keys[1], 1), 0, 1)
    brick_mask = draw_brick_mask(jax.random.fold_in(keys[6], 71), 0)
    owner = draw_owner(jax.random.fold_in(keys[6], 71), 0)
    weights = scatter_about(keys[4], (3, 3, 3, CIN, C), (27 * CIN) ** -0.5, 0.109375)
    bias = jnp.clip(jax.random.uniform(keys[5], (C,), jnp.float32, -0.5, 0.5), -0.5, 0.5)
    return {"features": features, "voxel_mask": voxel_mask, "brick_mask": brick_mask, "owner": owner, "weights": weights, "bias": bias}


def expand_bricks(brick_mask):
    grown = jnp.repeat(brick_mask, EDGE, axis=0)
    grown = jnp.repeat(grown, EDGE, axis=1)
    return jnp.repeat(grown, EDGE, axis=2)


def reference(features, voxel_mask, brick_mask, owner, weights, bias):
    live = voxel_mask * expand_bricks(brick_mask)
    inputs = features * live.astype(jnp.bfloat16)[..., None]
    padded = jnp.pad(inputs, ((1, 1), (1, 1), (1, 1), (0, 0)))
    kernel = weights.astype(jnp.float32)
    live_float = live.astype(jnp.float32)
    rows = BX * EDGE
    order = jnp.arange(BRICKS, dtype=jnp.int32)
    earlier = order[None, :] < order[:, None]

    def strip(index):
        piece = lax.dynamic_slice_in_dim(padded, index * rows, rows + 2, 0).astype(jnp.float32)
        pre = lax.conv_general_dilated(piece[None], kernel, (1, 1, 1), "VALID",
                                       dimension_numbers=("NDHWC", "DHWIO", "NCDHW"),
                                       precision=lax.Precision.HIGHEST)[0]
        mask_strip = lax.dynamic_slice_in_dim(live_float, index * rows, rows, 0)
        value = (jnp.maximum(pre + bias[:, None, None, None], 0.0) * mask_strip[None]).astype(jnp.bfloat16)
        value = value.reshape(C, BX, EDGE, N_GY, BY, EDGE, BZ, EDGE)
        value = value.transpose(3, 1, 4, 6, 0, 2, 5, 7).reshape(N_GY * BRICKS, C, EDGE**3)
        ids = lax.dynamic_index_in_dim(owner, index, 0, keepdims=False).reshape(N_GY, BRICKS)
        same = ids[:, :, None] == ids[:, None, :]
        rank = jnp.sum(jnp.logical_and(same, earlier[None]).astype(jnp.int32), axis=2)
        source = jnp.arange(N_GY, dtype=jnp.int32)[:, None]
        dest = ids * (N_GY * CAP) + source * CAP + rank
        empty = jnp.zeros((N_GY * N_GY * CAP, C, EDGE**3), jnp.bfloat16)
        return empty.at[dest.reshape(-1)].set(value)

    return lax.map(strip, jnp.arange(N_GX, dtype=jnp.int32))
```

```python
import jax
import jax.numpy as jnp
from jax import lax
from jax.sharding import PartitionSpec as P
from jax.experimental import pallas as pl
from jax.experimental.pallas import tpu as pltpu

C = 64
EDGE = 16


def padded_2(cells, sides, width):
    for axis, dim in sides:
        count = lax.axis_size(axis)
        ends = count - 1
        head = lax.slice_in_dim(cells, 0, width, axis=dim)
        tail = lax.slice_in_dim(cells, cells.shape[dim] - width, cells.shape[dim], axis=dim)
        cells = jnp.concatenate(
            [
                lax.ppermute(tail, axis, [(i, (i + 1) % count) for i in range(ends)]),
                cells,
                lax.ppermute(head, axis, [((i + 1) % count, i) for i in range(ends)]),
            ],
            axis=dim,
        )
    return cells


def conv_kernel(table_ref, x_ref, w_ref, b_ref, m_ref, o_ref):
    slot = pl.program_id(0)
    slots = pl.num_programs(0)
    valid = table_ref[slots + slot]
    rows = EDGE * EDGE

    @pl.when(valid > 0)
    def _():
        def body(ex, carry):
            acc = jnp.zeros((rows, C), jnp.float32)
            for a in range(3):
                for b in range(3):
                    lhs = x_ref[pl.ds(ex + a, 1), pl.ds(b, EDGE), :, :]
                    lhs = lhs.reshape(rows, lhs.shape[-1])
                    acc = acc + jnp.dot(lhs, w_ref[a * 3 + b], preferred_element_type=jnp.float32)
            start = pl.multiple_of(ex * rows, rows)
            mask = m_ref[0, :, pl.ds(start, rows)]
            value = jnp.maximum(acc.T + b_ref[...], 0.0) * mask
            o_ref[0, :, pl.ds(start, rows)] = value.astype(o_ref.dtype)
            return carry

        lax.fori_loop(0, EDGE, body, 0)

    @pl.when(valid == 0)
    def _():
        o_ref[...] = jnp.zeros(o_ref.shape, o_ref.dtype)


def conv_slots(table, shifted, w9, bias_col, masks, total, bricks_z):
    depth = shifted.shape[-1]
    span = shifted.shape[1]

    def brick_of(j, table_ref):
        return table_ref[j]

    def x_map(j, table_ref):
        brick = brick_of(j, table_ref)
        return (brick // bricks_z * EDGE, 0, brick % bricks_z * EDGE, 0)

    return pl.pallas_call(
        conv_kernel,
        out_shape=jax.ShapeDtypeStruct((total, C, EDGE**3), jnp.bfloat16),
        grid_spec=pltpu.PrefetchScalarGridSpec(
            num_scalar_prefetch=1,
            grid=(total,),
            in_specs=[
                pl.BlockSpec((pl.Element(EDGE + 2), pl.Element(span), pl.Element(EDGE), pl.Element(depth)), x_map),
                pl.BlockSpec(w9.shape, lambda j, t: (0, 0, 0)),
                pl.BlockSpec(bias_col.shape, lambda j, t: (0, 0)),
                pl.BlockSpec((1, 1, EDGE**3), lambda j, t: (brick_of(j, t), 0, 0)),
            ],
            out_specs=pl.BlockSpec((1, C, EDGE**3), lambda j, t: (j, 0, 0)),
        ),
        compiler_params=pltpu.CompilerParams(vmem_limit_bytes=48 * 1024 * 1024),
    )(table, shifted, w9, bias_col, masks)


def per_device(features, voxel_mask, brick_mask, owner, weights, bias):
    extent_x, extent_y, extent_z, channels_in = features.shape
    bricks_x = extent_x // EDGE
    bricks_y = extent_y // EDGE
    bricks_z = extent_z // EDGE
    count = bricks_x * bricks_y * bricks_z
    groups = lax.axis_size("gy")
    capacity = (count + groups - 1) // groups
    grown = jnp.repeat(brick_mask, EDGE, axis=0)
    grown = jnp.repeat(grown, EDGE, axis=1)
    grown = jnp.repeat(grown, EDGE, axis=2)
    live = (voxel_mask * grown).astype(jnp.bfloat16)
    inputs = features * live[..., None]
    padded = padded_2(inputs, (("gx", 0), ("gy", 1)), 1)
    padded = jnp.pad(padded, ((0, 0), (0, 0), (1, 1), (0, 0)))
    shifted = jnp.concatenate([padded[:, :, c:c + extent_z, :] for c in range(3)], axis=-1)
    brick_masks = live.astype(jnp.float32).reshape(bricks_x, EDGE, bricks_y, EDGE, bricks_z, EDGE)
    brick_masks = brick_masks.transpose(0, 2, 4, 1, 3, 5).reshape(count, 1, EDGE**3)
    ids = owner.reshape(count)
    order = jnp.arange(count, dtype=jnp.int32)
    same = ids[:, None] == ids[None, :]
    rank = jnp.sum(jnp.logical_and(same, order[None, :] < order[:, None]).astype(jnp.int32), axis=1)
    slots = ids * capacity + rank
    total = groups * capacity
    hit = slots[None, :] == jnp.arange(total, dtype=jnp.int32)[:, None]
    brick_of_slot = jnp.sum(jnp.where(hit, order[None, :], 0), axis=1)
    valid = jnp.any(hit, axis=1).astype(jnp.int32)
    table = jnp.concatenate([brick_of_slot, valid]).astype(jnp.int32)
    w9 = weights.reshape(9, 3 * channels_in, C)
    bias_col = bias.reshape(C, 1).astype(jnp.float32)
    sending = conv_slots(table, shifted, w9, bias_col, brick_masks, total, bricks_z)
    decoded = lax.all_to_all(sending, "gy", split_axis=0, concat_axis=0, tiled=True)
    return decoded[None]


def solution(mesh):
    return jax.shard_map(
        per_device,
        mesh=mesh,
        in_specs=(
            P("gx", "gy", None, None),
            P("gx", "gy", None),
            P("gx", "gy", None),
            P("gx", "gy", None, None),
            P(),
            P(),
        ),
        out_specs=P("gx", "gy", None, None),
        check_vma=False,
    )
```

```python
import jax
import jax.numpy as jnp
from jax import lax
from jax.sharding import PartitionSpec as P
from jax.experimental import pallas as pl
from jax.experimental.pallas import tpu as pltpu

C = 64
EDGE = 16


def padded_2(cells, sides, width):
    for axis, dim in sides:
        count = lax.axis_size(axis)
        ends = count - 1
        head = lax.slice_in_dim(cells, 0, width, axis=dim)
        tail = lax.slice_in_dim(cells, cells.shape[dim] - width, cells.shape[dim], axis=dim)
        cells = jnp.concatenate(
            [
                lax.ppermute(tail, axis, [(i, (i + 1) % count) for i in range(ends)]),
                cells,
                lax.ppermute(head, axis, [((i + 1) % count, i) for i in range(ends)]),
            ],
            axis=dim,
        )
    return cells


def conv_kernel(table_ref, x_ref, w_ref, b_ref, m_ref, o_ref, part_ref):
    slot = pl.program_id(0)
    slots = pl.num_programs(0)
    valid = table_ref[slots + slot]
    rows = EDGE * EDGE

    @pl.when(valid > 0)
    def _():
        def taps(xi, carry):
            part = jnp.zeros((rows, 3 * C), jnp.float32)
            for b in range(3):
                lhs = x_ref[pl.ds(xi, 1), pl.ds(b, EDGE), :, :]
                lhs = lhs.reshape(rows, lhs.shape[-1])
                part = part + jnp.dot(lhs, w_ref[b], preferred_element_type=jnp.float32)
            part_ref[xi] = part.T
            return carry

        lax.fori_loop(0, EDGE + 2, taps, 0)

        def rows_out(ex, carry):
            pre = (part_ref[ex, 0:C, :] + part_ref[ex + 1, C:2 * C, :]) + part_ref[ex + 2, 2 * C:3 * C, :]
            start = pl.multiple_of(ex * rows, rows)
            mask = m_ref[0, :, pl.ds(start, rows)]
            value = jnp.maximum(pre + b_ref[...], 0.0) * mask
            o_ref[0, :, pl.ds(start, rows)] = value.astype(o_ref.dtype)
            return carry

        lax.fori_loop(0, EDGE, rows_out, 0)

    @pl.when(valid == 0)
    def _():
        o_ref[...] = jnp.zeros(o_ref.shape, o_ref.dtype)


def conv_slots(table, shifted, w9, bias_col, masks, total, bricks_z):
    depth = shifted.shape[-1]
    span = shifted.shape[1]

    def brick_of(j, table_ref):
        return table_ref[j]

    def x_map(j, table_ref):
        brick = brick_of(j, table_ref)
        return (brick // bricks_z * EDGE, 0, brick % bricks_z * EDGE, 0)

    return pl.pallas_call(
        conv_kernel,
        out_shape=jax.ShapeDtypeStruct((total, C, EDGE**3), jnp.bfloat16),
        grid_spec=pltpu.PrefetchScalarGridSpec(
            num_scalar_prefetch=1,
            grid=(total,),
            in_specs=[
                pl.BlockSpec((pl.Element(EDGE + 2), pl.Element(span), pl.Element(EDGE), pl.Element(depth)), x_map),
                pl.BlockSpec(w9.shape, lambda j, t: (0, 0, 0)),
                pl.BlockSpec(bias_col.shape, lambda j, t: (0, 0)),
                pl.BlockSpec((1, 1, EDGE**3), lambda j, t: (brick_of(j, t), 0, 0)),
            ],
            out_specs=pl.BlockSpec((1, C, EDGE**3), lambda j, t: (j, 0, 0)),
            scratch_shapes=[pltpu.VMEM((EDGE + 2, 3 * C, EDGE * EDGE), jnp.float32)],
        ),
        compiler_params=pltpu.CompilerParams(vmem_limit_bytes=48 * 1024 * 1024),
    )(table, shifted, w9, bias_col, masks)


def per_device(features, voxel_mask, brick_mask, owner, weights, bias):
    extent_x, extent_y, extent_z, channels_in = features.shape
    bricks_x = extent_x // EDGE
    bricks_y = extent_y // EDGE
    bricks_z = extent_z // EDGE
    count = bricks_x * bricks_y * bricks_z
    groups = lax.axis_size("gy")
    capacity = (count + groups - 1) // groups
    grown = jnp.repeat(brick_mask, EDGE, axis=0)
    grown = jnp.repeat(grown, EDGE, axis=1)
    grown = jnp.repeat(grown, EDGE, axis=2)
    live = (voxel_mask * grown).astype(jnp.bfloat16)
    inputs = features * live[..., None]
    padded = padded_2(inputs, (("gx", 0), ("gy", 1)), 1)
    padded = jnp.pad(padded, ((0, 0), (0, 0), (1, 1), (0, 0)))
    shifted = jnp.concatenate([padded[:, :, c:c + extent_z, :] for c in range(3)], axis=-1)
    brick_masks = live.astype(jnp.float32).reshape(bricks_x, EDGE, bricks_y, EDGE, bricks_z, EDGE)
    brick_masks = brick_masks.transpose(0, 2, 4, 1, 3, 5).reshape(count, 1, EDGE**3)
    ids = owner.reshape(count)
    order = jnp.arange(count, dtype=jnp.int32)
    same = ids[:, None] == ids[None, :]
    rank = jnp.sum(jnp.logical_and(same, order[None, :] < order[:, None]).astype(jnp.int32), axis=1)
    slots = ids * capacity + rank
    total = groups * capacity
    hit = slots[None, :] == jnp.arange(total, dtype=jnp.int32)[:, None]
    brick_of_slot = jnp.sum(jnp.where(hit, order[None, :], 0), axis=1)
    valid = jnp.any(hit, axis=1).astype(jnp.int32)
    table = jnp.concatenate([brick_of_slot, valid]).astype(jnp.int32)
    w9 = weights.transpose(1, 2, 3, 0, 4).reshape(3, 3 * channels_in, 3 * C)
    bias_col = bias.reshape(C, 1).astype(jnp.float32)
    sending = conv_slots(table, shifted, w9, bias_col, brick_masks, total, bricks_z)
    decoded = lax.all_to_all(sending, "gy", split_axis=0, concat_axis=0, tiled=True)
    return decoded[None]


def solution(mesh):
    return jax.shard_map(
        per_device,
        mesh=mesh,
        in_specs=(
            P("gx", "gy", None, None),
            P("gx", "gy", None),
            P("gx", "gy", None),
            P("gx", "gy", None, None),
            P(),
            P(),
        ),
        out_specs=P("gx", "gy", None, None),
        check_vma=False,
    )
```

```python
import jax
import jax.numpy as jnp
from jax import lax
from jax.sharding import PartitionSpec as P
from jax.experimental import pallas as pl
from jax.experimental.pallas import tpu as pltpu

C = 64
EDGE = 16


def padded_2(cells, sides, width):
    for axis, dim in sides:
        count = lax.axis_size(axis)
        ends = count - 1
        head = lax.slice_in_dim(cells, 0, width, axis=dim)
        tail = lax.slice_in_dim(cells, cells.shape[dim] - width, cells.shape[dim], axis=dim)
        cells = jnp.concatenate(
            [
                lax.ppermute(tail, axis, [(i, (i + 1) % count) for i in range(ends)]),
                cells,
                lax.ppermute(head, axis, [((i + 1) % count, i) for i in range(ends)]),
            ],
            axis=dim,
        )
    return cells


def conv_kernel(table_ref, x_ref, w_ref, b_ref, m_ref, o_ref, part_ref):
    slot = pl.program_id(0)
    slots = pl.num_programs(0)
    valid = table_ref[slots + slot]
    rows = EDGE * EDGE
    group = 6
    chunk = 4 * rows

    @pl.when(valid > 0)
    def _():
        for first in range(0, EDGE + 2, group):
            part = jnp.zeros((group * rows, 3 * C), jnp.float32)
            for b in range(3):
                lhs = x_ref[first:first + group, b:b + EDGE, :, :]
                lhs = lhs.reshape(group * rows, lhs.shape[-1])
                part = part + jnp.dot(lhs, w_ref[b], preferred_element_type=jnp.float32)
            part_ref[:, first * rows:(first + group) * rows] = part.T

        def rows_out(piece, carry):
            start = pl.multiple_of(piece * chunk, chunk)
            pre = part_ref[0:C, pl.ds(start, chunk)]
            pre = pre + part_ref[C:2 * C, pl.ds(start + rows, chunk)]
            pre = pre + part_ref[2 * C:3 * C, pl.ds(start + 2 * rows, chunk)]
            mask = m_ref[0, :, pl.ds(start, chunk)]
            value = jnp.maximum(pre + b_ref[...], 0.0) * mask
            o_ref[0, :, pl.ds(start, chunk)] = value.astype(o_ref.dtype)
            return carry

        lax.fori_loop(0, EDGE**3 // chunk, rows_out, 0)

    @pl.when(valid == 0)
    def _():
        o_ref[...] = jnp.zeros(o_ref.shape, o_ref.dtype)


def conv_slots(table, shifted, w9, bias_col, masks, total, bricks_z):
    depth = shifted.shape[-1]
    span = shifted.shape[1]

    def brick_of(j, table_ref):
        return table_ref[j]

    def x_map(j, table_ref):
        brick = brick_of(j, table_ref)
        return (brick // bricks_z * EDGE, 0, brick % bricks_z * EDGE, 0)

    return pl.pallas_call(
        conv_kernel,
        out_shape=jax.ShapeDtypeStruct((total, C, EDGE**3), jnp.bfloat16),
        grid_spec=pltpu.PrefetchScalarGridSpec(
            num_scalar_prefetch=1,
            grid=(total,),
            in_specs=[
                pl.BlockSpec((pl.Element(EDGE + 2), pl.Element(span), pl.Element(EDGE), pl.Element(depth)), x_map),
                pl.BlockSpec(w9.shape, lambda j, t: (0, 0, 0)),
                pl.BlockSpec(bias_col.shape, lambda j, t: (0, 0)),
                pl.BlockSpec((1, 1, EDGE**3), lambda j, t: (brick_of(j, t), 0, 0)),
            ],
            out_specs=pl.BlockSpec((1, C, EDGE**3), lambda j, t: (j, 0, 0)),
            scratch_shapes=[pltpu.VMEM((3 * C, (EDGE + 2) * EDGE * EDGE), jnp.float32)],
        ),
        compiler_params=pltpu.CompilerParams(vmem_limit_bytes=48 * 1024 * 1024),
    )(table, shifted, w9, bias_col, masks)


def per_device(features, voxel_mask, brick_mask, owner, weights, bias):
    extent_x, extent_y, extent_z, channels_in = features.shape
    bricks_x = extent_x // EDGE
    bricks_y = extent_y // EDGE
    bricks_z = extent_z // EDGE
    count = bricks_x * bricks_y * bricks_z
    groups = lax.axis_size("gy")
    capacity = (count + groups - 1) // groups
    grown = jnp.repeat(brick_mask, EDGE, axis=0)
    grown = jnp.repeat(grown, EDGE, axis=1)
    grown = jnp.repeat(grown, EDGE, axis=2)
    live = (voxel_mask * grown).astype(jnp.bfloat16)
    inputs = features * live[..., None]
    padded = padded_2(inputs, (("gx", 0), ("gy", 1)), 1)
    padded = jnp.pad(padded, ((0, 0), (0, 0), (1, 1), (0, 0)))
    shifted = jnp.concatenate([padded[:, :, c:c + extent_z, :] for c in range(3)], axis=-1)
    brick_masks = live.astype(jnp.float32).reshape(bricks_x, EDGE, bricks_y, EDGE, bricks_z, EDGE)
    brick_masks = brick_masks.transpose(0, 2, 4, 1, 3, 5).reshape(count, 1, EDGE**3)
    ids = owner.reshape(count)
    order = jnp.arange(count, dtype=jnp.int32)
    same = ids[:, None] == ids[None, :]
    rank = jnp.sum(jnp.logical_and(same, order[None, :] < order[:, None]).astype(jnp.int32), axis=1)
    slots = ids * capacity + rank
    total = groups * capacity
    hit = slots[None, :] == jnp.arange(total, dtype=jnp.int32)[:, None]
    brick_of_slot = jnp.sum(jnp.where(hit, order[None, :], 0), axis=1)
    valid = jnp.any(hit, axis=1).astype(jnp.int32)
    table = jnp.concatenate([brick_of_slot, valid]).astype(jnp.int32)
    w9 = weights.transpose(1, 2, 3, 0, 4).reshape(3, 3 * channels_in, 3 * C)
    bias_col = bias.reshape(C, 1).astype(jnp.float32)
    sending = conv_slots(table, shifted, w9, bias_col, brick_masks, total, bricks_z)
    decoded = lax.all_to_all(sending, "gy", split_axis=0, concat_axis=0, tiled=True)
    return decoded[None]


def solution(mesh):
    return jax.shard_map(
        per_device,
        mesh=mesh,
        in_specs=(
            P("gx", "gy", None, None),
            P("gx", "gy", None),
            P("gx", "gy", None),
            P("gx", "gy", None, None),
            P(),
            P(),
        ),
        out_specs=P("gx", "gy", None, None),
        check_vma=False,
    )
```

```python
import jax
import jax.numpy as jnp
from jax import lax
from jax.sharding import PartitionSpec as P
from jax.experimental import pallas as pl
from jax.experimental.pallas import tpu as pltpu

C = 64
EDGE = 16


def padded_2(cells, sides, width):
    for axis, dim in sides:
        count = lax.axis_size(axis)
        ends = count - 1
        head = lax.slice_in_dim(cells, 0, width, axis=dim)
        tail = lax.slice_in_dim(cells, cells.shape[dim] - width, cells.shape[dim], axis=dim)
        cells = jnp.concatenate(
            [
                lax.ppermute(tail, axis, [(i, (i + 1) % count) for i in range(ends)]),
                cells,
                lax.ppermute(head, axis, [((i + 1) % count, i) for i in range(ends)]),
            ],
            axis=dim,
        )
    return cells


def conv_kernel(table_ref, x_ref, w_ref, b_ref, m_ref, o_ref, part_ref):
    slot = pl.program_id(0)
    slots = pl.num_programs(0)
    valid = table_ref[slots + slot]
    rows = EDGE * EDGE
    group = 6
    chunk = 4 * rows

    @pl.when(valid > 0)
    def _():
        for first in range(0, EDGE + 2, group):
            part = jnp.zeros((group * rows, 3 * C), jnp.float32)
            for b in range(3):
                lhs = x_ref[first:first + group, b:b + EDGE, :, :]
                lhs = lhs.reshape(group * rows, lhs.shape[-1])
                part = part + jnp.dot(lhs, w_ref[b], preferred_element_type=jnp.float32)
            part_ref[:, first * rows:(first + group) * rows] = part.T

        def rows_out(piece, carry):
            start = pl.multiple_of(piece * chunk, chunk)
            pre = part_ref[0:C, pl.ds(start, chunk)]
            pre = pre + part_ref[C:2 * C, pl.ds(start + rows, chunk)]
            pre = pre + part_ref[2 * C:3 * C, pl.ds(start + 2 * rows, chunk)]
            mask = m_ref[0, :, pl.ds(start, chunk)]
            value = jnp.maximum(pre + b_ref[...], 0.0) * mask
            o_ref[0, :, pl.ds(start, chunk)] = value.astype(o_ref.dtype)
            return carry

        lax.fori_loop(0, EDGE**3 // chunk, rows_out, 0)

    @pl.when(valid == 0)
    def _():
        o_ref[...] = jnp.zeros(o_ref.shape, o_ref.dtype)


def conv_slots(table, shifted, w9, bias_col, masks, total, bricks_z):
    depth = shifted.shape[-1]
    span = shifted.shape[1]

    def brick_of(j, table_ref):
        return table_ref[j]

    def x_map(j, table_ref):
        brick = brick_of(j, table_ref)
        return (brick // bricks_z * EDGE, 0, brick % bricks_z * EDGE, 0)

    return pl.pallas_call(
        conv_kernel,
        out_shape=jax.ShapeDtypeStruct((total, C, EDGE**3), jnp.bfloat16),
        grid_spec=pltpu.PrefetchScalarGridSpec(
            num_scalar_prefetch=1,
            grid=(total,),
            in_specs=[
                pl.BlockSpec((pl.Element(EDGE + 2), pl.Element(span), pl.Element(EDGE), pl.Element(depth)), x_map),
                pl.BlockSpec(w9.shape, lambda j, t: (0, 0, 0)),
                pl.BlockSpec(bias_col.shape, lambda j, t: (0, 0)),
                pl.BlockSpec((1, 1, EDGE**3), lambda j, t: (brick_of(j, t), 0, 0)),
            ],
            out_specs=pl.BlockSpec((1, C, EDGE**3), lambda j, t: (j, 0, 0)),
            scratch_shapes=[pltpu.VMEM((3 * C, (EDGE + 2) * EDGE * EDGE), jnp.float32)],
        ),
        compiler_params=pltpu.CompilerParams(vmem_limit_bytes=48 * 1024 * 1024),
        cost_estimate=pl.CostEstimate(
            flops=total * 2 * (EDGE + 2) * EDGE * EDGE * 9 * depth * C,
            bytes_accessed=total * (shifted.dtype.itemsize * (EDGE + 2) * span * EDGE * depth + 2 * C * EDGE**3),
            transcendentals=0,
        ),
    )(table, shifted, w9, bias_col, masks)


def per_device(features, voxel_mask, brick_mask, owner, weights, bias):
    extent_x, extent_y, extent_z, channels_in = features.shape
    bricks_x = extent_x // EDGE
    bricks_y = extent_y // EDGE
    bricks_z = extent_z // EDGE
    count = bricks_x * bricks_y * bricks_z
    groups = lax.axis_size("gy")
    capacity = (count + groups - 1) // groups
    grown = jnp.repeat(brick_mask, EDGE, axis=0)
    grown = jnp.repeat(grown, EDGE, axis=1)
    grown = jnp.repeat(grown, EDGE, axis=2)
    live = (voxel_mask * grown).astype(jnp.bfloat16)
    inputs = features * live[..., None]
    padded = padded_2(inputs, (("gx", 0), ("gy", 1)), 1)
    padded = jnp.pad(padded, ((0, 0), (0, 0), (1, 1), (0, 0)))
    shifted = jnp.concatenate([padded[:, :, c:c + extent_z, :] for c in range(3)], axis=-1)
    brick_masks = live.astype(jnp.float32).reshape(bricks_x, EDGE, bricks_y, EDGE, bricks_z, EDGE)
    brick_masks = brick_masks.transpose(0, 2, 4, 1, 3, 5).reshape(count, 1, EDGE**3)
    ids = owner.reshape(count)
    order = jnp.arange(count, dtype=jnp.int32)
    same = ids[:, None] == ids[None, :]
    rank = jnp.sum(jnp.logical_and(same, order[None, :] < order[:, None]).astype(jnp.int32), axis=1)
    slots = ids * capacity + rank
    total = groups * capacity
    hit = slots[None, :] == jnp.arange(total, dtype=jnp.int32)[:, None]
    brick_of_slot = jnp.sum(jnp.where(hit, order[None, :], 0), axis=1)
    valid = jnp.any(hit, axis=1).astype(jnp.int32)
    me = lax.axis_index("gy")
    w9 = weights.transpose(1, 2, 3, 0, 4).reshape(3, 3 * channels_in, 3 * C)
    bias_col = bias.reshape(C, 1).astype(jnp.float32)
    chunks = 4
    per_chunk = total // chunks
    received = []
    for m in range(chunks):
        shifts = jnp.arange(m * per_chunk, (m + 1) * per_chunk, dtype=jnp.int32)
        wanted = lax.rem(me + shifts, total)
        table = jnp.concatenate([brick_of_slot[wanted], valid[wanted]]).astype(jnp.int32)
        out = conv_slots(table, shifted, w9, bias_col, brick_masks, per_chunk, bricks_z)
        for i in range(per_chunk):
            k = m * per_chunk + i
            piece = out[i]
            if k:
                piece = lax.ppermute(piece, "gy", [(src, (src + k) % groups) for src in range(groups)])
            received.append(piece)
    flipped = jnp.stack([received[(-j) % total] for j in range(total)])
    decoded = jnp.roll(flipped, me, axis=0)
    return decoded[None]


def solution(mesh):
    return jax.shard_map(
        per_device,
        mesh=mesh,
        in_specs=(
            P("gx", "gy", None, None),
            P("gx", "gy", None),
            P("gx", "gy", None),
            P("gx", "gy", None, None),
            P(),
            P(),
        ),
        out_specs=P("gx", "gy", None, None),
        check_vma=False,
    )
```

```python
import jax
import jax.numpy as jnp
from jax import lax
from jax.sharding import PartitionSpec as P
from jax.experimental import pallas as pl
from jax.experimental.pallas import tpu as pltpu

C = 64
EDGE = 16


def padded_2(cells, sides, width):
    for axis, dim in sides:
        count = lax.axis_size(axis)
        ends = count - 1
        head = lax.slice_in_dim(cells, 0, width, axis=dim)
        tail = lax.slice_in_dim(cells, cells.shape[dim] - width, cells.shape[dim], axis=dim)
        cells = jnp.concatenate(
            [
                lax.ppermute(tail, axis, [(i, (i + 1) % count) for i in range(ends)]),
                cells,
                lax.ppermute(head, axis, [((i + 1) % count, i) for i in range(ends)]),
            ],
            axis=dim,
        )
    return cells


def conv_kernel(table_ref, x_ref, w_ref, b_ref, m_ref, o_ref, part_ref):
    slot = pl.program_id(0)
    slots = pl.num_programs(0)
    valid = table_ref[slots + slot]
    rows = EDGE * EDGE
    group = 6
    chunk = 4 * rows

    @pl.when(valid > 0)
    def _():
        for first in range(0, EDGE + 2, group):
            part = jnp.zeros((group * rows, 3 * C), jnp.float32)
            for b in range(3):
                lhs = jnp.concatenate(
                    [x_ref[first:first + group, b:b + EDGE, c:c + EDGE, :] for c in range(3)], axis=-1
                )
                lhs = lhs.reshape(group * rows, lhs.shape[-1])
                part = part + jnp.dot(lhs, w_ref[b], preferred_element_type=jnp.float32)
            part_ref[:, first * rows:(first + group) * rows] = part.T

        def rows_out(piece, carry):
            start = pl.multiple_of(piece * chunk, chunk)
            pre = part_ref[0:C, pl.ds(start, chunk)]
            pre = pre + part_ref[C:2 * C, pl.ds(start + rows, chunk)]
            pre = pre + part_ref[2 * C:3 * C, pl.ds(start + 2 * rows, chunk)]
            mask = m_ref[0, :, pl.ds(start, chunk)]
            value = jnp.maximum(pre + b_ref[...], 0.0) * mask
            o_ref[0, :, pl.ds(start, chunk)] = value.astype(o_ref.dtype)
            return carry

        lax.fori_loop(0, EDGE**3 // chunk, rows_out, 0)

    @pl.when(valid == 0)
    def _():
        o_ref[...] = jnp.zeros(o_ref.shape, o_ref.dtype)


def conv_slots(table, shifted, w9, bias_col, masks, total, bricks_z):
    depth = shifted.shape[-1]
    window = 2 * EDGE
    span = shifted.shape[1]

    def brick_of(j, table_ref):
        return table_ref[j]

    def x_map(j, table_ref):
        brick = brick_of(j, table_ref)
        return (brick // bricks_z * EDGE, 0, brick % bricks_z * EDGE, 0)

    return pl.pallas_call(
        conv_kernel,
        out_shape=jax.ShapeDtypeStruct((total, C, EDGE**3), jnp.bfloat16),
        grid_spec=pltpu.PrefetchScalarGridSpec(
            num_scalar_prefetch=1,
            grid=(total,),
            in_specs=[
                pl.BlockSpec((pl.Element(EDGE + 2), pl.Element(span), pl.Element(window), pl.Element(depth)), x_map),
                pl.BlockSpec(w9.shape, lambda j, t: (0, 0, 0)),
                pl.BlockSpec(bias_col.shape, lambda j, t: (0, 0)),
                pl.BlockSpec((1, 1, EDGE**3), lambda j, t: (brick_of(j, t), 0, 0)),
            ],
            out_specs=pl.BlockSpec((1, C, EDGE**3), lambda j, t: (j, 0, 0)),
            scratch_shapes=[pltpu.VMEM((3 * C, (EDGE + 2) * EDGE * EDGE), jnp.float32)],
        ),
        compiler_params=pltpu.CompilerParams(vmem_limit_bytes=48 * 1024 * 1024),
    )(table, shifted, w9, bias_col, masks)


def per_device(features, voxel_mask, brick_mask, owner, weights, bias):
    extent_x, extent_y, extent_z, channels_in = features.shape
    bricks_x = extent_x // EDGE
    bricks_y = extent_y // EDGE
    bricks_z = extent_z // EDGE
    count = bricks_x * bricks_y * bricks_z
    groups = lax.axis_size("gy")
    capacity = (count + groups - 1) // groups
    grown = jnp.repeat(brick_mask, EDGE, axis=0)
    grown = jnp.repeat(grown, EDGE, axis=1)
    grown = jnp.repeat(grown, EDGE, axis=2)
    live = (voxel_mask * grown).astype(jnp.bfloat16)
    inputs = features * live[..., None]
    padded = padded_2(inputs, (("gx", 0), ("gy", 1)), 1)
    shifted = jnp.pad(padded, ((0, 0), (0, 0), (1, EDGE - 1), (0, 0)))
    brick_masks = live.astype(jnp.float32).reshape(bricks_x, EDGE, bricks_y, EDGE, bricks_z, EDGE)
    brick_masks = brick_masks.transpose(0, 2, 4, 1, 3, 5).reshape(count, 1, EDGE**3)
    ids = owner.reshape(count)
    order = jnp.arange(count, dtype=jnp.int32)
    same = ids[:, None] == ids[None, :]
    rank = jnp.sum(jnp.logical_and(same, order[None, :] < order[:, None]).astype(jnp.int32), axis=1)
    slots = ids * capacity + rank
    total = groups * capacity
    hit = slots[None, :] == jnp.arange(total, dtype=jnp.int32)[:, None]
    brick_of_slot = jnp.sum(jnp.where(hit, order[None, :], 0), axis=1)
    valid = jnp.any(hit, axis=1).astype(jnp.int32)
    table = jnp.concatenate([brick_of_slot, valid]).astype(jnp.int32)
    w9 = weights.transpose(1, 2, 3, 0, 4).reshape(3, 3 * channels_in, 3 * C)
    bias_col = bias.reshape(C, 1).astype(jnp.float32)
    sending = conv_slots(table, shifted, w9, bias_col, brick_masks, total, bricks_z)
    decoded = lax.all_to_all(sending, "gy", split_axis=0, concat_axis=0, tiled=True)
    return decoded[None]


def solution(mesh):
    return jax.shard_map(
        per_device,
        mesh=mesh,
        in_specs=(
            P("gx", "gy", None, None),
            P("gx", "gy", None),
            P("gx", "gy", None),
            P("gx", "gy", None, None),
            P(),
            P(),
        ),
        out_specs=P("gx", "gy", None, None),
        check_vma=False,
    )
```

```python
import jax
import jax.numpy as jnp
from jax import lax
from jax.sharding import PartitionSpec as P
from jax.experimental import pallas as pl
from jax.experimental.pallas import tpu as pltpu

C = 64
EDGE = 16


def shift(piece, axes, steps):
    sizes = [lax.axis_size(axis) for axis in axes]
    total = 1
    for size in sizes:
        total *= size
    pairs = []
    for source in range(total):
        place = []
        rest = source
        for size in reversed(sizes):
            place.append(rest % size)
            rest //= size
        place = place[::-1]
        moved = [p + d for p, d in zip(place, steps)]
        if all(0 <= m < size for m, size in zip(moved, sizes)):
            target = 0
            for m, size in zip(moved, sizes):
                target = target * size + m
            pairs.append((source, target))
    return lax.ppermute(piece, axes if len(axes) > 1 else axes[0], pairs)


def padded_2(cells):
    both = ("gx", "gy")
    up = shift(cells[-1:], ("gx",), (1,))
    down = shift(cells[:1], ("gx",), (-1,))
    left = shift(cells[:, -1:], ("gy",), (1,))
    right = shift(cells[:, :1], ("gy",), (-1,))
    up_left = shift(cells[-1:, -1:], both, (1, 1))
    up_right = shift(cells[-1:, :1], both, (1, -1))
    down_left = shift(cells[:1, -1:], both, (-1, 1))
    down_right = shift(cells[:1, :1], both, (-1, -1))
    top = jnp.concatenate([up_left, up, up_right], axis=1)
    middle = jnp.concatenate([left, cells, right], axis=1)
    bottom = jnp.concatenate([down_left, down, down_right], axis=1)
    return jnp.concatenate([top, middle, bottom], axis=0)


def conv_kernel(table_ref, x_ref, w_ref, b_ref, m_ref, o_ref, part_ref):
    slot = pl.program_id(0)
    slots = pl.num_programs(0)
    valid = table_ref[slots + slot]
    rows = EDGE * EDGE
    group = 6
    chunk = 4 * rows

    @pl.when(valid > 0)
    def _():
        for first in range(0, EDGE + 2, group):
            part = jnp.zeros((group * rows, 3 * C), jnp.float32)
            for b in range(3):
                lhs = jnp.concatenate(
                    [x_ref[first:first + group, b:b + EDGE, c:c + EDGE, :] for c in range(3)], axis=-1
                )
                lhs = lhs.reshape(group * rows, lhs.shape[-1])
                part = part + jnp.dot(lhs, w_ref[b], preferred_element_type=jnp.float32)
            part_ref[:, first * rows:(first + group) * rows] = part.T

        def rows_out(piece, carry):
            start = pl.multiple_of(piece * chunk, chunk)
            pre = part_ref[0:C, pl.ds(start, chunk)]
            pre = pre + part_ref[C:2 * C, pl.ds(start + rows, chunk)]
            pre = pre + part_ref[2 * C:3 * C, pl.ds(start + 2 * rows, chunk)]
            mask = m_ref[0, :, pl.ds(start, chunk)]
            value = jnp.maximum(pre + b_ref[...], 0.0) * mask
            o_ref[0, :, pl.ds(start, chunk)] = value.astype(o_ref.dtype)
            return carry

        lax.fori_loop(0, EDGE**3 // chunk, rows_out, 0)

    @pl.when(valid == 0)
    def _():
        o_ref[...] = jnp.zeros(o_ref.shape, o_ref.dtype)


def conv_slots(table, shifted, w9, bias_col, masks, total, bricks_z):
    depth = shifted.shape[-1]
    window = 2 * EDGE
    span = shifted.shape[1]

    def brick_of(j, table_ref):
        return table_ref[j]

    def x_map(j, table_ref):
        brick = brick_of(j, table_ref)
        return (brick // bricks_z * EDGE, 0, brick % bricks_z * EDGE, 0)

    return pl.pallas_call(
        conv_kernel,
        out_shape=jax.ShapeDtypeStruct((total, C, EDGE**3), jnp.bfloat16),
        grid_spec=pltpu.PrefetchScalarGridSpec(
            num_scalar_prefetch=1,
            grid=(total,),
            in_specs=[
                pl.BlockSpec((pl.Element(EDGE + 2), pl.Element(span), pl.Element(window), pl.Element(depth)), x_map),
                pl.BlockSpec(w9.shape, lambda j, t: (0, 0, 0)),
                pl.BlockSpec(bias_col.shape, lambda j, t: (0, 0)),
                pl.BlockSpec((1, 1, EDGE**3), lambda j, t: (brick_of(j, t), 0, 0)),
            ],
            out_specs=pl.BlockSpec((1, C, EDGE**3), lambda j, t: (j, 0, 0)),
            scratch_shapes=[pltpu.VMEM((3 * C, (EDGE + 2) * EDGE * EDGE), jnp.float32)],
        ),
        compiler_params=pltpu.CompilerParams(vmem_limit_bytes=48 * 1024 * 1024),
    )(table, shifted, w9, bias_col, masks)


def per_device(features, voxel_mask, brick_mask, owner, weights, bias):
    extent_x, extent_y, extent_z, channels_in = features.shape
    bricks_x = extent_x // EDGE
    bricks_y = extent_y // EDGE
    bricks_z = extent_z // EDGE
    count = bricks_x * bricks_y * bricks_z
    groups = lax.axis_size("gy")
    capacity = (count + groups - 1) // groups
    grown = jnp.repeat(brick_mask, EDGE, axis=0)
    grown = jnp.repeat(grown, EDGE, axis=1)
    grown = jnp.repeat(grown, EDGE, axis=2)
    live = (voxel_mask * grown).astype(jnp.bfloat16)
    inputs = features * live[..., None]
    padded = padded_2(inputs)
    shifted = jnp.pad(padded, ((0, 0), (0, 0), (1, EDGE - 1), (0, 0)))
    brick_masks = live.astype(jnp.float32).reshape(bricks_x, EDGE, bricks_y, EDGE, bricks_z, EDGE)
    brick_masks = brick_masks.transpose(0, 2, 4, 1, 3, 5).reshape(count, 1, EDGE**3)
    ids = owner.reshape(count)
    order = jnp.arange(count, dtype=jnp.int32)
    same = ids[:, None] == ids[None, :]
    rank = jnp.sum(jnp.logical_and(same, order[None, :] < order[:, None]).astype(jnp.int32), axis=1)
    slots = ids * capacity + rank
    total = groups * capacity
    hit = slots[None, :] == jnp.arange(total, dtype=jnp.int32)[:, None]
    brick_of_slot = jnp.sum(jnp.where(hit, order[None, :], 0), axis=1)
    valid = jnp.any(hit, axis=1).astype(jnp.int32)
    table = jnp.concatenate([brick_of_slot, valid]).astype(jnp.int32)
    w9 = weights.transpose(1, 2, 3, 0, 4).reshape(3, 3 * channels_in, 3 * C)
    bias_col = bias.reshape(C, 1).astype(jnp.float32)
    sending = conv_slots(table, shifted, w9, bias_col, brick_masks, total, bricks_z)
    decoded = lax.all_to_all(sending, "gy", split_axis=0, concat_axis=0, tiled=True)
    return decoded[None]


def solution(mesh):
    return jax.shard_map(
        per_device,
        mesh=mesh,
        in_specs=(
            P("gx", "gy", None, None),
            P("gx", "gy", None),
            P("gx", "gy", None),
            P("gx", "gy", None, None),
            P(),
            P(),
        ),
        out_specs=P("gx", "gy", None, None),
        check_vma=False,
    )
```

```python
import jax
import jax.numpy as jnp
from jax import lax
from jax.sharding import PartitionSpec as P
from jax.experimental import pallas as pl
from jax.experimental.pallas import tpu as pltpu

C = 64
EDGE = 16


def padded_2(cells, sides, width):
    for axis, dim in sides:
        count = lax.axis_size(axis)
        ends = count - 1
        head = lax.slice_in_dim(cells, 0, width, axis=dim)
        tail = lax.slice_in_dim(cells, cells.shape[dim] - width, cells.shape[dim], axis=dim)
        cells = jnp.concatenate(
            [
                lax.ppermute(tail, axis, [(i, (i + 1) % count) for i in range(ends)]),
                cells,
                lax.ppermute(head, axis, [((i + 1) % count, i) for i in range(ends)]),
            ],
            axis=dim,
        )
    return cells


def conv_kernel(table_ref, x_ref, w_ref, b_ref, m_ref, o_ref, part_ref):
    slot = pl.program_id(0)
    slots = pl.num_programs(0)
    valid = table_ref[slots + slot]
    rows = EDGE * EDGE
    group = 9
    chunk = 4 * rows

    @pl.when(valid > 0)
    def _():
        for first in range(0, EDGE + 2, group):
            part = jnp.zeros((group * rows, 3 * C), jnp.float32)
            for b in range(3):
                lhs = jnp.concatenate(
                    [x_ref[first:first + group, b:b + EDGE, c:c + EDGE, :] for c in range(3)], axis=-1
                )
                lhs = lhs.reshape(group * rows, lhs.shape[-1])
                part = part + jnp.dot(lhs, w_ref[b], preferred_element_type=jnp.float32)
            part_ref[:, first * rows:(first + group) * rows] = part.T

        def rows_out(piece, carry):
            start = pl.multiple_of(piece * chunk, chunk)
            pre = part_ref[0:C, pl.ds(start, chunk)]
            pre = pre + part_ref[C:2 * C, pl.ds(start + rows, chunk)]
            pre = pre + part_ref[2 * C:3 * C, pl.ds(start + 2 * rows, chunk)]
            mask = m_ref[0, :, pl.ds(start, chunk)]
            value = jnp.maximum(pre + b_ref[...], 0.0) * mask
            o_ref[0, :, pl.ds(start, chunk)] = value.astype(o_ref.dtype)
            return carry

        lax.fori_loop(0, EDGE**3 // chunk, rows_out, 0)

    @pl.when(valid == 0)
    def _():
        o_ref[...] = jnp.zeros(o_ref.shape, o_ref.dtype)


def conv_slots(table, shifted, w9, bias_col, masks, total, bricks_z):
    depth = shifted.shape[-1]
    window = 2 * EDGE
    span = shifted.shape[1]

    def brick_of(j, table_ref):
        return table_ref[j]

    def x_map(j, table_ref):
        brick = brick_of(j, table_ref)
        return (brick // bricks_z * EDGE, 0, brick % bricks_z * EDGE, 0)

    return pl.pallas_call(
        conv_kernel,
        out_shape=jax.ShapeDtypeStruct((total, C, EDGE**3), jnp.bfloat16),
        grid_spec=pltpu.PrefetchScalarGridSpec(
            num_scalar_prefetch=1,
            grid=(total,),
            in_specs=[
                pl.BlockSpec((pl.Element(EDGE + 2), pl.Element(span), pl.Element(window), pl.Element(depth)), x_map),
                pl.BlockSpec(w9.shape, lambda j, t: (0, 0, 0)),
                pl.BlockSpec(bias_col.shape, lambda j, t: (0, 0)),
                pl.BlockSpec((1, 1, EDGE**3), lambda j, t: (brick_of(j, t), 0, 0)),
            ],
            out_specs=pl.BlockSpec((1, C, EDGE**3), lambda j, t: (j, 0, 0)),
            scratch_shapes=[pltpu.VMEM((3 * C, (EDGE + 2) * EDGE * EDGE), jnp.float32)],
        ),
        compiler_params=pltpu.CompilerParams(vmem_limit_bytes=48 * 1024 * 1024),
    )(table, shifted, w9, bias_col, masks)


def per_device(features, voxel_mask, brick_mask, owner, weights, bias):
    extent_x, extent_y, extent_z, channels_in = features.shape
    bricks_x = extent_x // EDGE
    bricks_y = extent_y // EDGE
    bricks_z = extent_z // EDGE
    count = bricks_x * bricks_y * bricks_z
    groups = lax.axis_size("gy")
    capacity = (count + groups - 1) // groups
    grown = jnp.repeat(brick_mask, EDGE, axis=0)
    grown = jnp.repeat(grown, EDGE, axis=1)
    grown = jnp.repeat(grown, EDGE, axis=2)
    live = (voxel_mask * grown).astype(jnp.bfloat16)
    inputs = features * live[..., None]
    padded = padded_2(inputs, (("gx", 0), ("gy", 1)), 1)
    shifted = jnp.pad(padded, ((0, 0), (0, 0), (1, EDGE - 1), (0, 0)))
    brick_masks = live.astype(jnp.float32).reshape(bricks_x, EDGE, bricks_y, EDGE, bricks_z, EDGE)
    brick_masks = brick_masks.transpose(0, 2, 4, 1, 3, 5).reshape(count, 1, EDGE**3)
    ids = owner.reshape(count)
    order = jnp.arange(count, dtype=jnp.int32)
    same = ids[:, None] == ids[None, :]
    rank = jnp.sum(jnp.logical_and(same, order[None, :] < order[:, None]).astype(jnp.int32), axis=1)
    slots = ids * capacity + rank
    total = groups * capacity
    hit = slots[None, :] == jnp.arange(total, dtype=jnp.int32)[:, None]
    brick_of_slot = jnp.sum(jnp.where(hit, order[None, :], 0), axis=1)
    valid = jnp.any(hit, axis=1).astype(jnp.int32)
    table = jnp.concatenate([brick_of_slot, valid]).astype(jnp.int32)
    w9 = weights.transpose(1, 2, 3, 0, 4).reshape(3, 3 * channels_in, 3 * C)
    bias_col = bias.reshape(C, 1).astype(jnp.float32)
    sending = conv_slots(table, shifted, w9, bias_col, brick_masks, total, bricks_z)
    decoded = lax.all_to_all(sending, "gy", split_axis=0, concat_axis=0, tiled=True)
    return decoded[None]


def solution(mesh):
    return jax.shard_map(
        per_device,
        mesh=mesh,
        in_specs=(
            P("gx", "gy", None, None),
            P("gx", "gy", None),
            P("gx", "gy", None),
            P("gx", "gy", None, None),
            P(),
            P(),
        ),
        out_specs=P("gx", "gy", None, None),
        check_vma=False,
    )
```

```python
import jax
import jax.numpy as jnp
from jax import lax
from jax.sharding import PartitionSpec as P
from jax.experimental import pallas as pl
from jax.experimental.pallas import tpu as pltpu

C = 64
EDGE = 16


def padded_2(cells, sides, width):
    for axis, dim in sides:
        count = lax.axis_size(axis)
        ends = count - 1
        head = lax.slice_in_dim(cells, 0, width, axis=dim)
        tail = lax.slice_in_dim(cells, cells.shape[dim] - width, cells.shape[dim], axis=dim)
        cells = jnp.concatenate(
            [
                lax.ppermute(tail, axis, [(i, (i + 1) % count) for i in range(ends)]),
                cells,
                lax.ppermute(head, axis, [((i + 1) % count, i) for i in range(ends)]),
            ],
            axis=dim,
        )
    return cells


def conv_kernel(table_ref, x_ref, w_ref, b_ref, m_ref, o_ref, part_ref):
    slot = pl.program_id(0)
    slots = pl.num_programs(0)
    valid = table_ref[slots + slot]
    rows = EDGE * EDGE
    group = 6
    chunk = 4 * rows

    @pl.when(valid > 0)
    def _():
        for first in range(0, EDGE + 2, group):
            part = jnp.zeros((group * rows, 3 * C), jnp.float32)
            for b in range(3):
                lhs = jnp.concatenate(
                    [x_ref[first:first + group, b:b + EDGE, c:c + EDGE, :] for c in range(3)], axis=-1
                )
                lhs = lhs.reshape(group * rows, lhs.shape[-1])
                part = part + jnp.dot(lhs, w_ref[b], preferred_element_type=jnp.float32)
            part_ref[:, first * rows:(first + group) * rows] = part.T

        def rows_out(piece, carry):
            start = pl.multiple_of(piece * chunk, chunk)
            pre = part_ref[0:C, pl.ds(start, chunk)]
            pre = pre + part_ref[C:2 * C, pl.ds(start + rows, chunk)]
            pre = pre + part_ref[2 * C:3 * C, pl.ds(start + 2 * rows, chunk)]
            mask = m_ref[0, :, pl.ds(start, chunk)]
            value = jnp.maximum(pre + b_ref[...], 0.0) * mask
            o_ref[0, :, pl.ds(start, chunk)] = value.astype(o_ref.dtype)
            return carry

        lax.fori_loop(0, EDGE**3 // chunk, rows_out, 0)

    @pl.when(valid == 0)
    def _():
        o_ref[...] = jnp.zeros(o_ref.shape, o_ref.dtype)


def conv_slots(table, shifted, w9, bias_col, masks, total, bricks_z):
    depth = shifted.shape[-1]
    window = 2 * EDGE
    span = shifted.shape[1]

    def brick_of(j, table_ref):
        return table_ref[j]

    def x_map(j, table_ref):
        brick = brick_of(j, table_ref)
        return (brick // bricks_z * EDGE, 0, brick % bricks_z * EDGE, 0)

    return pl.pallas_call(
        conv_kernel,
        out_shape=jax.ShapeDtypeStruct((total, C, EDGE**3), jnp.bfloat16),
        grid_spec=pltpu.PrefetchScalarGridSpec(
            num_scalar_prefetch=1,
            grid=(total,),
            in_specs=[
                pl.BlockSpec((pl.Element(EDGE + 2), pl.Element(span), pl.Element(window), pl.Element(depth)), x_map),
                pl.BlockSpec(w9.shape, lambda j, t: (0, 0, 0)),
                pl.BlockSpec(bias_col.shape, lambda j, t: (0, 0)),
                pl.BlockSpec((1, 1, EDGE**3), lambda j, t: (brick_of(j, t), 0, 0)),
            ],
            out_specs=pl.BlockSpec((1, C, EDGE**3), lambda j, t: (j, 0, 0)),
            scratch_shapes=[pltpu.VMEM((3 * C, (EDGE + 2) * EDGE * EDGE), jnp.float32)],
        ),
        compiler_params=pltpu.CompilerParams(vmem_limit_bytes=48 * 1024 * 1024),
    )(table, shifted, w9, bias_col, masks)


def per_device(features, voxel_mask, brick_mask, owner, weights, bias):
    extent_x, extent_y, extent_z, channels_in = features.shape
    bricks_x = extent_x // EDGE
    bricks_y = extent_y // EDGE
    bricks_z = extent_z // EDGE
    count = bricks_x * bricks_y * bricks_z
    groups = lax.axis_size("gy")
    capacity = (count + groups - 1) // groups
    grown = jnp.repeat(brick_mask, EDGE, axis=0)
    grown = jnp.repeat(grown, EDGE, axis=1)
    grown = jnp.repeat(grown, EDGE, axis=2)
    live = (voxel_mask * grown).astype(jnp.bfloat16)
    inputs = features * live[..., None]
    padded = padded_2(inputs, (("gx", 0), ("gy", 1)), 1)
    shifted = jnp.pad(padded, ((0, 0), (0, 0), (1, EDGE - 1), (0, 0)))
    brick_masks = live.astype(jnp.float32).reshape(bricks_x, EDGE, bricks_y, EDGE, bricks_z, EDGE)
    brick_masks = brick_masks.transpose(0, 2, 4, 1, 3, 5).reshape(count, 1, EDGE**3)
    ids = owner.reshape(count)
    order = jnp.arange(count, dtype=jnp.int32)
    same = ids[:, None] == ids[None, :]
    rank = jnp.sum(jnp.logical_and(same, order[None, :] < order[:, None]).astype(jnp.int32), axis=1)
    slots = ids * capacity + rank
    total = groups * capacity
    hit = slots[None, :] == jnp.arange(total, dtype=jnp.int32)[:, None]
    brick_of_slot = jnp.sum(jnp.where(hit, order[None, :], 0), axis=1)
    valid = jnp.any(hit, axis=1).astype(jnp.int32)
    seen = lax.cummax(jnp.where(valid > 0, jnp.arange(total, dtype=jnp.int32), -1))
    first = jnp.argmax(valid)
    held = jnp.where(seen >= 0, brick_of_slot[jnp.maximum(seen, 0)], brick_of_slot[first])
    table = jnp.concatenate([held, valid]).astype(jnp.int32)
    w9 = weights.transpose(1, 2, 3, 0, 4).reshape(3, 3 * channels_in, 3 * C)
    bias_col = bias.reshape(C, 1).astype(jnp.float32)
    sending = conv_slots(table, shifted, w9, bias_col, brick_masks, total, bricks_z)
    decoded = lax.all_to_all(sending, "gy", split_axis=0, concat_axis=0, tiled=True)
    return decoded[None]


def solution(mesh):
    return jax.shard_map(
        per_device,
        mesh=mesh,
        in_specs=(
            P("gx", "gy", None, None),
            P("gx", "gy", None),
            P("gx", "gy", None),
            P("gx", "gy", None, None),
            P(),
            P(),
        ),
        out_specs=P("gx", "gy", None, None),
        check_vma=False,
    )
```

```python
import jax
import jax.numpy as jnp
from jax import lax
from jax.sharding import PartitionSpec as P
from jax.experimental import pallas as pl
from jax.experimental.pallas import tpu as pltpu

C = 64
EDGE = 16


def padded_2(cells, sides, width):
    for axis, dim in sides:
        count = lax.axis_size(axis)
        ends = count - 1
        head = lax.slice_in_dim(cells, 0, width, axis=dim)
        tail = lax.slice_in_dim(cells, cells.shape[dim] - width, cells.shape[dim], axis=dim)
        cells = jnp.concatenate(
            [
                lax.ppermute(tail, axis, [(i, (i + 1) % count) for i in range(ends)]),
                cells,
                lax.ppermute(head, axis, [((i + 1) % count, i) for i in range(ends)]),
            ],
            axis=dim,
        )
    return cells


def conv_kernel(table_ref, x_ref, w_ref, b_ref, m_ref, o_ref, part_ref):
    slot = pl.program_id(0)
    slots = pl.num_programs(0)
    valid = table_ref[slots + slot]
    rows = EDGE * EDGE
    group = 3
    chunk = 4 * rows

    @pl.when(valid > 0)
    def _():
        for first in range(0, EDGE + 2, group):
            part = jnp.zeros((group * rows, 3 * C), jnp.float32)
            for b in range(3):
                lhs = jnp.concatenate(
                    [x_ref[first:first + group, b:b + EDGE, c:c + EDGE, :] for c in range(3)], axis=-1
                )
                lhs = lhs.reshape(group * rows, lhs.shape[-1])
                part = part + jnp.dot(lhs, w_ref[b], preferred_element_type=jnp.float32)
            part_ref[:, first * rows:(first + group) * rows] = part.T

        def rows_out(piece, carry):
            start = pl.multiple_of(piece * chunk, chunk)
            pre = part_ref[0:C, pl.ds(start, chunk)]
            pre = pre + part_ref[C:2 * C, pl.ds(start + rows, chunk)]
            pre = pre + part_ref[2 * C:3 * C, pl.ds(start + 2 * rows, chunk)]
            mask = m_ref[0, :, pl.ds(start, chunk)]
            value = jnp.maximum(pre + b_ref[...], 0.0) * mask
            o_ref[0, :, pl.ds(start, chunk)] = value.astype(o_ref.dtype)
            return carry

        lax.fori_loop(0, EDGE**3 // chunk, rows_out, 0)

    @pl.when(valid == 0)
    def _():
        o_ref[...] = jnp.zeros(o_ref.shape, o_ref.dtype)


def conv_slots(table, shifted, w9, bias_col, masks, total, bricks_z):
    depth = shifted.shape[-1]
    window = 2 * EDGE
    span = shifted.shape[1]

    def brick_of(j, table_ref):
        return table_ref[j]

    def x_map(j, table_ref):
        brick = brick_of(j, table_ref)
        return (brick // bricks_z * EDGE, 0, brick % bricks_z * EDGE, 0)

    return pl.pallas_call(
        conv_kernel,
        out_shape=jax.ShapeDtypeStruct((total, C, EDGE**3), jnp.bfloat16),
        grid_spec=pltpu.PrefetchScalarGridSpec(
            num_scalar_prefetch=1,
            grid=(total,),
            in_specs=[
                pl.BlockSpec((pl.Element(EDGE + 2), pl.Element(span), pl.Element(window), pl.Element(depth)), x_map),
                pl.BlockSpec(w9.shape, lambda j, t: (0, 0, 0)),
                pl.BlockSpec(bias_col.shape, lambda j, t: (0, 0)),
                pl.BlockSpec((1, 1, EDGE**3), lambda j, t: (brick_of(j, t), 0, 0)),
            ],
            out_specs=pl.BlockSpec((1, C, EDGE**3), lambda j, t: (j, 0, 0)),
            scratch_shapes=[pltpu.VMEM((3 * C, (EDGE + 2) * EDGE * EDGE), jnp.float32)],
        ),
        compiler_params=pltpu.CompilerParams(vmem_limit_bytes=48 * 1024 * 1024),
    )(table, shifted, w9, bias_col, masks)


def per_device(features, voxel_mask, brick_mask, owner, weights, bias):
    extent_x, extent_y, extent_z, channels_in = features.shape
    bricks_x = extent_x // EDGE
    bricks_y = extent_y // EDGE
    bricks_z = extent_z // EDGE
    count = bricks_x * bricks_y * bricks_z
    groups = lax.axis_size("gy")
    capacity = (count + groups - 1) // groups
    grown = jnp.repeat(brick_mask, EDGE, axis=0)
    grown = jnp.repeat(grown, EDGE, axis=1)
    grown = jnp.repeat(grown, EDGE, axis=2)
    live = (voxel_mask * grown).astype(jnp.bfloat16)
    inputs = features * live[..., None]
    padded = padded_2(inputs, (("gx", 0), ("gy", 1)), 1)
    shifted = jnp.pad(padded, ((0, 0), (0, 0), (1, EDGE - 1), (0, 0)))
    brick_masks = live.astype(jnp.float32).reshape(bricks_x, EDGE, bricks_y, EDGE, bricks_z, EDGE)
    brick_masks = brick_masks.transpose(0, 2, 4, 1, 3, 5).reshape(count, 1, EDGE**3)
    ids = owner.reshape(count)
    order = jnp.arange(count, dtype=jnp.int32)
    same = ids[:, None] == ids[None, :]
    rank = jnp.sum(jnp.logical_and(same, order[None, :] < order[:, None]).astype(jnp.int32), axis=1)
    slots = ids * capacity + rank
    total = groups * capacity
    hit = slots[None, :] == jnp.arange(total, dtype=jnp.int32)[:, None]
    brick_of_slot = jnp.sum(jnp.where(hit, order[None, :], 0), axis=1)
    valid = jnp.any(hit, axis=1).astype(jnp.int32)
    table = jnp.concatenate([brick_of_slot, valid]).astype(jnp.int32)
    w9 = weights.transpose(1, 2, 3, 0, 4).reshape(3, 3 * channels_in, 3 * C)
    bias_col = bias.reshape(C, 1).astype(jnp.float32)
    sending = conv_slots(table, shifted, w9, bias_col, brick_masks, total, bricks_z)
    decoded = lax.all_to_all(sending, "gy", split_axis=0, concat_axis=0, tiled=True)
    return decoded[None]


def solution(mesh):
    return jax.shard_map(
        per_device,
        mesh=mesh,
        in_specs=(
            P("gx", "gy", None, None),
            P("gx", "gy", None),
            P("gx", "gy", None),
            P("gx", "gy", None, None),
            P(),
            P(),
        ),
        out_specs=P("gx", "gy", None, None),
        check_vma=False,
    )
```

```python
import jax
import numpy as np
import jax.numpy as jnp
from jax import lax
from jax.sharding import PartitionSpec as P
from jax.experimental import pallas as pl
from jax.experimental.pallas import tpu as pltpu

C = 64
EDGE = 16


def padded_2(cells, sides, width):
    for axis, dim in sides:
        count = lax.axis_size(axis)
        ends = count - 1
        head = lax.slice_in_dim(cells, 0, width, axis=dim)
        tail = lax.slice_in_dim(cells, cells.shape[dim] - width, cells.shape[dim], axis=dim)
        cells = jnp.concatenate(
            [
                lax.ppermute(tail, axis, [(i, (i + 1) % count) for i in range(ends)]),
                cells,
                lax.ppermute(head, axis, [((i + 1) % count, i) for i in range(ends)]),
            ],
            axis=dim,
        )
    return cells


def conv_kernel(table_ref, x_ref, w_ref, b_ref, m_ref, o_ref, part_ref):
    slot = pl.program_id(0)
    slots = pl.num_programs(0)
    valid = table_ref[slots + slot]
    rows = EDGE * EDGE
    group = 6
    chunk = 4 * rows

    @pl.when(valid > 0)
    def _():
        for first in range(0, EDGE + 2, group):
            part = jnp.zeros((group * rows, 3 * C), jnp.float32)
            for b in range(3):
                lhs = jnp.concatenate(
                    [x_ref[first:first + group, b:b + EDGE, c:c + EDGE, :] for c in range(3)], axis=-1
                )
                lhs = lhs.reshape(group * rows, lhs.shape[-1])
                part = part + jnp.dot(lhs, w_ref[b], preferred_element_type=jnp.float32)
            part_ref[:, first * rows:(first + group) * rows] = part.T

        def rows_out(piece, carry):
            start = pl.multiple_of(piece * chunk, chunk)
            pre = part_ref[0:C, pl.ds(start, chunk)]
            pre = pre + part_ref[C:2 * C, pl.ds(start + rows, chunk)]
            pre = pre + part_ref[2 * C:3 * C, pl.ds(start + 2 * rows, chunk)]
            mask = m_ref[0, :, pl.ds(start, chunk)]
            value = jnp.maximum(pre + b_ref[...], 0.0) * mask
            o_ref[0, :, pl.ds(start, chunk)] = value.astype(o_ref.dtype)
            return carry

        lax.fori_loop(0, EDGE**3 // chunk, rows_out, 0)

    @pl.when(valid == 0)
    def _():
        o_ref[...] = jnp.zeros(o_ref.shape, o_ref.dtype)


def conv_slots(table, shifted, w9, bias_col, masks, total, bricks_z):
    depth = shifted.shape[-1]
    window = 2 * EDGE
    span = shifted.shape[1]

    def brick_of(j, table_ref):
        return table_ref[j]

    def x_map(j, table_ref):
        brick = brick_of(j, table_ref)
        return (brick // bricks_z * EDGE, 0, brick % bricks_z * EDGE, 0)

    return pl.pallas_call(
        conv_kernel,
        out_shape=jax.ShapeDtypeStruct((total, C, EDGE**3), jnp.bfloat16),
        grid_spec=pltpu.PrefetchScalarGridSpec(
            num_scalar_prefetch=1,
            grid=(total,),
            in_specs=[
                pl.BlockSpec((pl.Element(EDGE + 2), pl.Element(span), pl.Element(window), pl.Element(depth)), x_map),
                pl.BlockSpec(w9.shape, lambda j, t: (0, 0, 0)),
                pl.BlockSpec(bias_col.shape, lambda j, t: (0, 0)),
                pl.BlockSpec((1, 1, EDGE**3), lambda j, t: (brick_of(j, t), 0, 0)),
            ],
            out_specs=pl.BlockSpec((1, C, EDGE**3), lambda j, t: (j, 0, 0)),
            scratch_shapes=[pltpu.VMEM((3 * C, (EDGE + 2) * EDGE * EDGE), jnp.float32)],
        ),
        compiler_params=pltpu.CompilerParams(vmem_limit_bytes=48 * 1024 * 1024),
    )(table, shifted, w9, bias_col, masks)


def per_device(features, voxel_mask, brick_mask, owner, weights, bias):
    extent_x, extent_y, extent_z, channels_in = features.shape
    bricks_x = extent_x // EDGE
    bricks_y = extent_y // EDGE
    bricks_z = extent_z // EDGE
    count = bricks_x * bricks_y * bricks_z
    groups = lax.axis_size("gy")
    capacity = (count + groups - 1) // groups
    grown = jnp.repeat(brick_mask, EDGE, axis=0)
    grown = jnp.repeat(grown, EDGE, axis=1)
    grown = jnp.repeat(grown, EDGE, axis=2)
    live = (voxel_mask * grown).astype(jnp.bfloat16)
    def masked(index):
        edge = features[index].astype(jnp.float32) * live[index].astype(jnp.float32)[..., None]
        return edge.astype(features.dtype)

    rows_x = lax.axis_size("gx")
    cols_y = lax.axis_size("gy")
    up = lax.ppermute(masked(np.s_[-1:]), "gx", [(i, i + 1) for i in range(rows_x - 1)])
    down = lax.ppermute(masked(np.s_[:1]), "gx", [(i + 1, i) for i in range(rows_x - 1)])
    extended = jnp.concatenate([up, features * live[..., None], down], axis=0)
    col_tail = jnp.concatenate([up[:, -1:], masked(np.s_[:, -1:]), down[:, -1:]], axis=0)
    col_head = jnp.concatenate([up[:, :1], masked(np.s_[:, :1]), down[:, :1]], axis=0)
    left = lax.ppermute(col_tail, "gy", [(i, i + 1) for i in range(cols_y - 1)])
    right = lax.ppermute(col_head, "gy", [(i + 1, i) for i in range(cols_y - 1)])
    padded = jnp.concatenate([left, extended, right], axis=1)
    shifted = jnp.pad(padded, ((0, 0), (0, 0), (1, EDGE - 1), (0, 0)))
    brick_masks = live.astype(jnp.float32).reshape(bricks_x, EDGE, bricks_y, EDGE, bricks_z, EDGE)
    brick_masks = brick_masks.transpose(0, 2, 4, 1, 3, 5).reshape(count, 1, EDGE**3)
    ids = owner.reshape(count)
    order = jnp.arange(count, dtype=jnp.int32)
    same = ids[:, None] == ids[None, :]
    rank = jnp.sum(jnp.logical_and(same, order[None, :] < order[:, None]).astype(jnp.int32), axis=1)
    slots = ids * capacity + rank
    total = groups * capacity
    hit = slots[None, :] == jnp.arange(total, dtype=jnp.int32)[:, None]
    brick_of_slot = jnp.sum(jnp.where(hit, order[None, :], 0), axis=1)
    valid = jnp.any(hit, axis=1).astype(jnp.int32)
    table = jnp.concatenate([brick_of_slot, valid]).astype(jnp.int32)
    w9 = weights.transpose(1, 2, 3, 0, 4).reshape(3, 3 * channels_in, 3 * C)
    bias_col = bias.reshape(C, 1).astype(jnp.float32)
    sending = conv_slots(table, shifted, w9, bias_col, brick_masks, total, bricks_z)
    decoded = lax.all_to_all(sending, "gy", split_axis=0, concat_axis=0, tiled=True)
    return decoded[None]


def solution(mesh):
    return jax.shard_map(
        per_device,
        mesh=mesh,
        in_specs=(
            P("gx", "gy", None, None),
            P("gx", "gy", None),
            P("gx", "gy", None),
            P("gx", "gy", None, None),
            P(),
            P(),
        ),
        out_specs=P("gx", "gy", None, None),
        check_vma=False,
    )
```

```python
import jax
import numpy as np
import jax.numpy as jnp
from jax import lax
from jax.sharding import PartitionSpec as P
from jax.experimental import pallas as pl
from jax.experimental.pallas import tpu as pltpu

C = 64
EDGE = 16


def padded_2(cells, sides, width):
    for axis, dim in sides:
        count = lax.axis_size(axis)
        ends = count - 1
        head = lax.slice_in_dim(cells, 0, width, axis=dim)
        tail = lax.slice_in_dim(cells, cells.shape[dim] - width, cells.shape[dim], axis=dim)
        cells = jnp.concatenate(
            [
                lax.ppermute(tail, axis, [(i, (i + 1) % count) for i in range(ends)]),
                cells,
                lax.ppermute(head, axis, [((i + 1) % count, i) for i in range(ends)]),
            ],
            axis=dim,
        )
    return cells


def shift(piece, axes, steps):
    sizes = [lax.axis_size(axis) for axis in axes]
    total = 1
    for size in sizes:
        total *= size
    pairs = []
    for source in range(total):
        place = []
        rest = source
        for size in reversed(sizes):
            place.append(rest % size)
            rest //= size
        place = place[::-1]
        moved = [p + d for p, d in zip(place, steps)]
        if all(0 <= m < size for m, size in zip(moved, sizes)):
            target = 0
            for m, size in zip(moved, sizes):
                target = target * size + m
            pairs.append((source, target))
    return lax.ppermute(piece, axes if len(axes) > 1 else axes[0], pairs)


def conv_kernel(table_ref, x_ref, w_ref, b_ref, m_ref, o_ref, part_ref):
    slot = pl.program_id(0)
    slots = pl.num_programs(0)
    valid = table_ref[slots + slot]
    rows = EDGE * EDGE
    group = 6
    chunk = 4 * rows

    @pl.when(valid > 0)
    def _():
        for first in range(0, EDGE + 2, group):
            part = jnp.zeros((group * rows, 3 * C), jnp.float32)
            for b in range(3):
                lhs = jnp.concatenate(
                    [x_ref[first:first + group, b:b + EDGE, c:c + EDGE, :] for c in range(3)], axis=-1
                )
                lhs = lhs.reshape(group * rows, lhs.shape[-1])
                part = part + jnp.dot(lhs, w_ref[b], preferred_element_type=jnp.float32)
            part_ref[:, first * rows:(first + group) * rows] = part.T

        def rows_out(piece, carry):
            start = pl.multiple_of(piece * chunk, chunk)
            pre = part_ref[0:C, pl.ds(start, chunk)]
            pre = pre + part_ref[C:2 * C, pl.ds(start + rows, chunk)]
            pre = pre + part_ref[2 * C:3 * C, pl.ds(start + 2 * rows, chunk)]
            mask = m_ref[0, :, pl.ds(start, chunk)]
            value = jnp.maximum(pre + b_ref[...], 0.0) * mask
            o_ref[0, :, pl.ds(start, chunk)] = value.astype(o_ref.dtype)
            return carry

        lax.fori_loop(0, EDGE**3 // chunk, rows_out, 0)

    @pl.when(valid == 0)
    def _():
        o_ref[...] = jnp.zeros(o_ref.shape, o_ref.dtype)


def conv_slots(table, shifted, w9, bias_col, masks, total, bricks_z):
    depth = shifted.shape[-1]
    window = 2 * EDGE
    span = shifted.shape[1]

    def brick_of(j, table_ref):
        return table_ref[j]

    def x_map(j, table_ref):
        brick = brick_of(j, table_ref)
        return (brick // bricks_z * EDGE, 0, brick % bricks_z * EDGE, 0)

    return pl.pallas_call(
        conv_kernel,
        out_shape=jax.ShapeDtypeStruct((total, C, EDGE**3), jnp.bfloat16),
        grid_spec=pltpu.PrefetchScalarGridSpec(
            num_scalar_prefetch=1,
            grid=(total,),
            in_specs=[
                pl.BlockSpec((pl.Element(EDGE + 2), pl.Element(span), pl.Element(window), pl.Element(depth)), x_map),
                pl.BlockSpec(w9.shape, lambda j, t: (0, 0, 0)),
                pl.BlockSpec(bias_col.shape, lambda j, t: (0, 0)),
                pl.BlockSpec((1, 1, EDGE**3), lambda j, t: (brick_of(j, t), 0, 0)),
            ],
            out_specs=pl.BlockSpec((1, C, EDGE**3), lambda j, t: (j, 0, 0)),
            scratch_shapes=[pltpu.VMEM((3 * C, (EDGE + 2) * EDGE * EDGE), jnp.float32)],
        ),
        compiler_params=pltpu.CompilerParams(vmem_limit_bytes=48 * 1024 * 1024),
    )(table, shifted, w9, bias_col, masks)


def per_device(features, voxel_mask, brick_mask, owner, weights, bias):
    extent_x, extent_y, extent_z, channels_in = features.shape
    bricks_x = extent_x // EDGE
    bricks_y = extent_y // EDGE
    bricks_z = extent_z // EDGE
    count = bricks_x * bricks_y * bricks_z
    groups = lax.axis_size("gy")
    capacity = (count + groups - 1) // groups
    grown = jnp.repeat(brick_mask, EDGE, axis=0)
    grown = jnp.repeat(grown, EDGE, axis=1)
    grown = jnp.repeat(grown, EDGE, axis=2)
    live = (voxel_mask * grown).astype(jnp.bfloat16)
    def masked(index):
        edge = features[index].astype(jnp.float32) * live[index].astype(jnp.float32)[..., None]
        return edge.astype(features.dtype)

    rows_x = lax.axis_size("gx")
    cols_y = lax.axis_size("gy")
    up = lax.ppermute(masked(np.s_[-1:]), "gx", [(i, i + 1) for i in range(rows_x - 1)])
    down = lax.ppermute(masked(np.s_[:1]), "gx", [(i + 1, i) for i in range(rows_x - 1)])
    extended = jnp.concatenate([up, features * live[..., None], down], axis=0)
    both = ("gx", "gy")
    left = lax.ppermute(masked(np.s_[:, -1:]), "gy", [(i, i + 1) for i in range(cols_y - 1)])
    right = lax.ppermute(masked(np.s_[:, :1]), "gy", [(i + 1, i) for i in range(cols_y - 1)])
    up_left = shift(masked(np.s_[-1:, -1:]), both, (1, 1))
    up_right = shift(masked(np.s_[-1:, :1]), both, (1, -1))
    down_left = shift(masked(np.s_[:1, -1:]), both, (-1, 1))
    down_right = shift(masked(np.s_[:1, :1]), both, (-1, -1))
    left = jnp.concatenate([up_left, left, down_left], axis=0)
    right = jnp.concatenate([up_right, right, down_right], axis=0)
    padded = jnp.concatenate([left, extended, right], axis=1)
    shifted = jnp.pad(padded, ((0, 0), (0, 0), (1, EDGE - 1), (0, 0)))
    brick_masks = live.astype(jnp.float32).reshape(bricks_x, EDGE, bricks_y, EDGE, bricks_z, EDGE)
    brick_masks = brick_masks.transpose(0, 2, 4, 1, 3, 5).reshape(count, 1, EDGE**3)
    ids = owner.reshape(count)
    order = jnp.arange(count, dtype=jnp.int32)
    same = ids[:, None] == ids[None, :]
    rank = jnp.sum(jnp.logical_and(same, order[None, :] < order[:, None]).astype(jnp.int32), axis=1)
    slots = ids * capacity + rank
    total = groups * capacity
    hit = slots[None, :] == jnp.arange(total, dtype=jnp.int32)[:, None]
    brick_of_slot = jnp.sum(jnp.where(hit, order[None, :], 0), axis=1)
    valid = jnp.any(hit, axis=1).astype(jnp.int32)
    table = jnp.concatenate([brick_of_slot, valid]).astype(jnp.int32)
    w9 = weights.transpose(1, 2, 3, 0, 4).reshape(3, 3 * channels_in, 3 * C)
    bias_col = bias.reshape(C, 1).astype(jnp.float32)
    sending = conv_slots(table, shifted, w9, bias_col, brick_masks, total, bricks_z)
    decoded = lax.all_to_all(sending, "gy", split_axis=0, concat_axis=0, tiled=True)
    return decoded[None]


def solution(mesh):
    return jax.shard_map(
        per_device,
        mesh=mesh,
        in_specs=(
            P("gx", "gy", None, None),
            P("gx", "gy", None),
            P("gx", "gy", None),
            P("gx", "gy", None, None),
            P(),
            P(),
        ),
        out_specs=P("gx", "gy", None, None),
        check_vma=False,
    )
```

```python
import jax
import numpy as np
import jax.numpy as jnp
from jax import lax
from jax.sharding import PartitionSpec as P
from jax.experimental import pallas as pl
from jax.experimental.pallas import tpu as pltpu

C = 64
EDGE = 16


def padded_2(cells, sides, width):
    for axis, dim in sides:
        count = lax.axis_size(axis)
        ends = count - 1
        head = lax.slice_in_dim(cells, 0, width, axis=dim)
        tail = lax.slice_in_dim(cells, cells.shape[dim] - width, cells.shape[dim], axis=dim)
        cells = jnp.concatenate(
            [
                lax.ppermute(tail, axis, [(i, (i + 1) % count) for i in range(ends)]),
                cells,
                lax.ppermute(head, axis, [((i + 1) % count, i) for i in range(ends)]),
            ],
            axis=dim,
        )
    return cells


def conv_kernel(table_ref, x_ref, w_ref, b_ref, m_ref, o_ref, part_ref):
    slot = pl.program_id(0)
    slots = pl.num_programs(0)
    valid = table_ref[slots + slot]
    rows = EDGE * EDGE
    group = 6
    chunk = 4 * rows

    @pl.when(valid > 0)
    def _():
        for first in range(0, EDGE + 2, group):
            lhs = jnp.concatenate(
                [x_ref[first:first + group, b:b + EDGE, c:c + EDGE, :] for b in range(3) for c in range(3)],
                axis=-1,
            )
            lhs = lhs.reshape(group * rows, lhs.shape[-1])
            part = jnp.dot(lhs, w_ref[...], preferred_element_type=jnp.float32)
            part_ref[:, first * rows:(first + group) * rows] = part.T

        def rows_out(piece, carry):
            start = pl.multiple_of(piece * chunk, chunk)
            pre = part_ref[0:C, pl.ds(start, chunk)]
            pre = pre + part_ref[C:2 * C, pl.ds(start + rows, chunk)]
            pre = pre + part_ref[2 * C:3 * C, pl.ds(start + 2 * rows, chunk)]
            mask = m_ref[0, :, pl.ds(start, chunk)]
            value = jnp.maximum(pre + b_ref[...], 0.0) * mask
            o_ref[0, :, pl.ds(start, chunk)] = value.astype(o_ref.dtype)
            return carry

        lax.fori_loop(0, EDGE**3 // chunk, rows_out, 0)

    @pl.when(valid == 0)
    def _():
        o_ref[...] = jnp.zeros(o_ref.shape, o_ref.dtype)


def conv_slots(table, shifted, w9, bias_col, masks, total, bricks_z):
    depth = shifted.shape[-1]
    window = 2 * EDGE
    span = shifted.shape[1]

    def brick_of(j, table_ref):
        return table_ref[j]

    def x_map(j, table_ref):
        brick = brick_of(j, table_ref)
        return (brick // bricks_z * EDGE, 0, brick % bricks_z * EDGE, 0)

    return pl.pallas_call(
        conv_kernel,
        out_shape=jax.ShapeDtypeStruct((total, C, EDGE**3), jnp.bfloat16),
        grid_spec=pltpu.PrefetchScalarGridSpec(
            num_scalar_prefetch=1,
            grid=(total,),
            in_specs=[
                pl.BlockSpec((pl.Element(EDGE + 2), pl.Element(span), pl.Element(window), pl.Element(depth)), x_map),
                pl.BlockSpec(w9.shape, lambda j, t: (0, 0)),
                pl.BlockSpec(bias_col.shape, lambda j, t: (0, 0)),
                pl.BlockSpec((1, 1, EDGE**3), lambda j, t: (brick_of(j, t), 0, 0)),
            ],
            out_specs=pl.BlockSpec((1, C, EDGE**3), lambda j, t: (j, 0, 0)),
            scratch_shapes=[pltpu.VMEM((3 * C, (EDGE + 2) * EDGE * EDGE), jnp.float32)],
        ),
        compiler_params=pltpu.CompilerParams(vmem_limit_bytes=48 * 1024 * 1024),
    )(table, shifted, w9, bias_col, masks)


def per_device(features, voxel_mask, brick_mask, owner, weights, bias):
    extent_x, extent_y, extent_z, channels_in = features.shape
    bricks_x = extent_x // EDGE
    bricks_y = extent_y // EDGE
    bricks_z = extent_z // EDGE
    count = bricks_x * bricks_y * bricks_z
    groups = lax.axis_size("gy")
    capacity = (count + groups - 1) // groups
    grown = jnp.repeat(brick_mask, EDGE, axis=0)
    grown = jnp.repeat(grown, EDGE, axis=1)
    grown = jnp.repeat(grown, EDGE, axis=2)
    live = (voxel_mask * grown).astype(jnp.bfloat16)
    def masked(index):
        edge = features[index].astype(jnp.float32) * live[index].astype(jnp.float32)[..., None]
        return edge.astype(features.dtype)

    rows_x = lax.axis_size("gx")
    cols_y = lax.axis_size("gy")
    up = lax.ppermute(masked(np.s_[-1:]), "gx", [(i, i + 1) for i in range(rows_x - 1)])
    down = lax.ppermute(masked(np.s_[:1]), "gx", [(i + 1, i) for i in range(rows_x - 1)])
    extended = jnp.concatenate([up, features * live[..., None], down], axis=0)
    col_tail = jnp.concatenate([up[:, -1:], masked(np.s_[:, -1:]), down[:, -1:]], axis=0)
    col_head = jnp.concatenate([up[:, :1], masked(np.s_[:, :1]), down[:, :1]], axis=0)
    left = lax.ppermute(col_tail, "gy", [(i, i + 1) for i in range(cols_y - 1)])
    right = lax.ppermute(col_head, "gy", [(i + 1, i) for i in range(cols_y - 1)])
    padded = jnp.concatenate([left, extended, right], axis=1)
    shifted = jnp.pad(padded, ((0, 0), (0, 0), (1, EDGE - 1), (0, 0)))
    brick_masks = live.astype(jnp.float32).reshape(bricks_x, EDGE, bricks_y, EDGE, bricks_z, EDGE)
    brick_masks = brick_masks.transpose(0, 2, 4, 1, 3, 5).reshape(count, 1, EDGE**3)
    ids = owner.reshape(count)
    order = jnp.arange(count, dtype=jnp.int32)
    same = ids[:, None] == ids[None, :]
    rank = jnp.sum(jnp.logical_and(same, order[None, :] < order[:, None]).astype(jnp.int32), axis=1)
    slots = ids * capacity + rank
    total = groups * capacity
    hit = slots[None, :] == jnp.arange(total, dtype=jnp.int32)[:, None]
    brick_of_slot = jnp.sum(jnp.where(hit, order[None, :], 0), axis=1)
    valid = jnp.any(hit, axis=1).astype(jnp.int32)
    table = jnp.concatenate([brick_of_slot, valid]).astype(jnp.int32)
    w9 = weights.transpose(1, 2, 3, 0, 4).reshape(9 * channels_in, 3 * C)
    bias_col = bias.reshape(C, 1).astype(jnp.float32)
    sending = conv_slots(table, shifted, w9, bias_col, brick_masks, total, bricks_z)
    decoded = lax.all_to_all(sending, "gy", split_axis=0, concat_axis=0, tiled=True)
    return decoded[None]


def solution(mesh):
    return jax.shard_map(
        per_device,
        mesh=mesh,
        in_specs=(
            P("gx", "gy", None, None),
            P("gx", "gy", None),
            P("gx", "gy", None),
            P("gx", "gy", None, None),
            P(),
            P(),
        ),
        out_specs=P("gx", "gy", None, None),
        check_vma=False,
    )
```

```python
import jax
import numpy as np
import jax.numpy as jnp
from jax import lax
from jax.sharding import PartitionSpec as P
from jax.experimental import pallas as pl
from jax.experimental.pallas import tpu as pltpu

C = 64
EDGE = 16


def padded_2(cells, sides, width):
    for axis, dim in sides:
        count = lax.axis_size(axis)
        ends = count - 1
        head = lax.slice_in_dim(cells, 0, width, axis=dim)
        tail = lax.slice_in_dim(cells, cells.shape[dim] - width, cells.shape[dim], axis=dim)
        cells = jnp.concatenate(
            [
                lax.ppermute(tail, axis, [(i, (i + 1) % count) for i in range(ends)]),
                cells,
                lax.ppermute(head, axis, [((i + 1) % count, i) for i in range(ends)]),
            ],
            axis=dim,
        )
    return cells


def conv_kernel(table_ref, x_ref, w_ref, b_ref, m_ref, o_ref, part_ref):
    slot = pl.program_id(0)
    slots = pl.num_programs(0)
    valid = table_ref[slots + slot]
    rows = EDGE * EDGE
    group = 9
    chunk = 4 * rows

    @pl.when(valid > 0)
    def _():
        for first in range(0, EDGE + 2, group):
            lhs = jnp.concatenate(
                [x_ref[first:first + group, b:b + EDGE, c:c + EDGE, :] for b in range(3) for c in range(3)],
                axis=-1,
            )
            lhs = lhs.reshape(group * rows, lhs.shape[-1])
            part = jnp.dot(lhs, w_ref[...], preferred_element_type=jnp.float32)
            part_ref[:, first * rows:(first + group) * rows] = part.T

        def rows_out(piece, carry):
            start = pl.multiple_of(piece * chunk, chunk)
            pre = part_ref[0:C, pl.ds(start, chunk)]
            pre = pre + part_ref[C:2 * C, pl.ds(start + rows, chunk)]
            pre = pre + part_ref[2 * C:3 * C, pl.ds(start + 2 * rows, chunk)]
            mask = m_ref[0, :, pl.ds(start, chunk)]
            value = jnp.maximum(pre + b_ref[...], 0.0) * mask
            o_ref[0, :, pl.ds(start, chunk)] = value.astype(o_ref.dtype)
            return carry

        lax.fori_loop(0, EDGE**3 // chunk, rows_out, 0)

    @pl.when(valid == 0)
    def _():
        o_ref[...] = jnp.zeros(o_ref.shape, o_ref.dtype)


def conv_slots(table, shifted, w9, bias_col, masks, total, bricks_z):
    depth = shifted.shape[-1]
    window = 2 * EDGE
    span = shifted.shape[1]

    def brick_of(j, table_ref):
        return table_ref[j]

    def x_map(j, table_ref):
        brick = brick_of(j, table_ref)
        return (brick // bricks_z * EDGE, 0, brick % bricks_z * EDGE, 0)

    return pl.pallas_call(
        conv_kernel,
        out_shape=jax.ShapeDtypeStruct((total, C, EDGE**3), jnp.bfloat16),
        grid_spec=pltpu.PrefetchScalarGridSpec(
            num_scalar_prefetch=1,
            grid=(total,),
            in_specs=[
                pl.BlockSpec((pl.Element(EDGE + 2), pl.Element(span), pl.Element(window), pl.Element(depth)), x_map),
                pl.BlockSpec(w9.shape, lambda j, t: (0, 0)),
                pl.BlockSpec(bias_col.shape, lambda j, t: (0, 0)),
                pl.BlockSpec((1, 1, EDGE**3), lambda j, t: (brick_of(j, t), 0, 0)),
            ],
            out_specs=pl.BlockSpec((1, C, EDGE**3), lambda j, t: (j, 0, 0)),
            scratch_shapes=[pltpu.VMEM((3 * C, (EDGE + 2) * EDGE * EDGE), jnp.float32)],
        ),
        compiler_params=pltpu.CompilerParams(vmem_limit_bytes=48 * 1024 * 1024),
    )(table, shifted, w9, bias_col, masks)


def per_device(features, voxel_mask, brick_mask, owner, weights, bias):
    extent_x, extent_y, extent_z, channels_in = features.shape
    bricks_x = extent_x // EDGE
    bricks_y = extent_y // EDGE
    bricks_z = extent_z // EDGE
    count = bricks_x * bricks_y * bricks_z
    groups = lax.axis_size("gy")
    capacity = (count + groups - 1) // groups
    grown = jnp.repeat(brick_mask, EDGE, axis=0)
    grown = jnp.repeat(grown, EDGE, axis=1)
    grown = jnp.repeat(grown, EDGE, axis=2)
    live = (voxel_mask * grown).astype(jnp.bfloat16)
    def masked(index):
        edge = features[index].astype(jnp.float32) * live[index].astype(jnp.float32)[..., None]
        return edge.astype(features.dtype)

    rows_x = lax.axis_size("gx")
    cols_y = lax.axis_size("gy")
    up = lax.ppermute(masked(np.s_[-1:]), "gx", [(i, i + 1) for i in range(rows_x - 1)])
    down = lax.ppermute(masked(np.s_[:1]), "gx", [(i + 1, i) for i in range(rows_x - 1)])
    extended = jnp.concatenate([up, features * live[..., None], down], axis=0)
    col_tail = jnp.concatenate([up[:, -1:], masked(np.s_[:, -1:]), down[:, -1:]], axis=0)
    col_head = jnp.concatenate([up[:, :1], masked(np.s_[:, :1]), down[:, :1]], axis=0)
    left = lax.ppermute(col_tail, "gy", [(i, i + 1) for i in range(cols_y - 1)])
    right = lax.ppermute(col_head, "gy", [(i + 1, i) for i in range(cols_y - 1)])
    padded = jnp.concatenate([left, extended, right], axis=1)
    shifted = jnp.pad(padded, ((0, 0), (0, 0), (1, EDGE - 1), (0, 0)))
    brick_masks = live.astype(jnp.float32).reshape(bricks_x, EDGE, bricks_y, EDGE, bricks_z, EDGE)
    brick_masks = brick_masks.transpose(0, 2, 4, 1, 3, 5).reshape(count, 1, EDGE**3)
    ids = owner.reshape(count)
    order = jnp.arange(count, dtype=jnp.int32)
    same = ids[:, None] == ids[None, :]
    rank = jnp.sum(jnp.logical_and(same, order[None, :] < order[:, None]).astype(jnp.int32), axis=1)
    slots = ids * capacity + rank
    total = groups * capacity
    hit = slots[None, :] == jnp.arange(total, dtype=jnp.int32)[:, None]
    brick_of_slot = jnp.sum(jnp.where(hit, order[None, :], 0), axis=1)
    valid = jnp.any(hit, axis=1).astype(jnp.int32)
    table = jnp.concatenate([brick_of_slot, valid]).astype(jnp.int32)
    w9 = weights.transpose(1, 2, 3, 0, 4).reshape(9 * channels_in, 3 * C)
    bias_col = bias.reshape(C, 1).astype(jnp.float32)
    sending = conv_slots(table, shifted, w9, bias_col, brick_masks, total, bricks_z)
    decoded = lax.all_to_all(sending, "gy", split_axis=0, concat_axis=0, tiled=True)
    return decoded[None]


def solution(mesh):
    return jax.shard_map(
        per_device,
        mesh=mesh,
        in_specs=(
            P("gx", "gy", None, None),
            P("gx", "gy", None),
            P("gx", "gy", None),
            P("gx", "gy", None, None),
            P(),
            P(),
        ),
        out_specs=P("gx", "gy", None, None),
        check_vma=False,
    )
```

```python
import jax
import numpy as np
import jax.numpy as jnp
from jax import lax
from jax.sharding import PartitionSpec as P
from jax.experimental import pallas as pl
from jax.experimental.pallas import tpu as pltpu

C = 64
EDGE = 16


def padded_2(cells, sides, width):
    for axis, dim in sides:
        count = lax.axis_size(axis)
        ends = count - 1
        head = lax.slice_in_dim(cells, 0, width, axis=dim)
        tail = lax.slice_in_dim(cells, cells.shape[dim] - width, cells.shape[dim], axis=dim)
        cells = jnp.concatenate(
            [
                lax.ppermute(tail, axis, [(i, (i + 1) % count) for i in range(ends)]),
                cells,
                lax.ppermute(head, axis, [((i + 1) % count, i) for i in range(ends)]),
            ],
            axis=dim,
        )
    return cells


def conv_kernel(table_ref, x_ref, w_ref, b_ref, m_ref, o_ref, part_ref):
    slot = pl.program_id(0)
    slots = pl.num_programs(0)
    valid = table_ref[slots + slot]
    rows = EDGE * EDGE
    group = 6
    chunk = 4 * rows

    @pl.when(valid > 0)
    def _():
        for first in range(0, EDGE + 2, group):
            lhs = jnp.concatenate(
                [x_ref[first:first + group, b:b + EDGE, c:c + EDGE, :] for b in range(3) for c in range(3)],
                axis=-1,
            )
            lhs = lhs.reshape(group * rows, lhs.shape[-1])
            part = jnp.dot(lhs, w_ref[...], preferred_element_type=jnp.float32)
            part_ref[:, first * rows:(first + group) * rows] = part.T

        def rows_out(piece, carry):
            start = pl.multiple_of(piece * chunk, chunk)
            pre = part_ref[0:C, pl.ds(start, chunk)]
            pre = pre + part_ref[C:2 * C, pl.ds(start + rows, chunk)]
            pre = pre + part_ref[2 * C:3 * C, pl.ds(start + 2 * rows, chunk)]
            mask = m_ref[0, :, pl.ds(start, chunk)]
            value = jnp.maximum(pre + b_ref[...], 0.0) * mask
            o_ref[0, :, pl.ds(start, chunk)] = value.astype(o_ref.dtype)
            return carry

        lax.fori_loop(0, EDGE**3 // chunk, rows_out, 0)

    @pl.when(valid == 0)
    def _():
        o_ref[...] = jnp.zeros(o_ref.shape, o_ref.dtype)


def conv_slots(table, shifted, w9, bias_col, masks, total, bricks_z):
    depth = shifted.shape[-1]
    window = 2 * EDGE
    span = shifted.shape[1]

    def brick_of(j, table_ref):
        return table_ref[j]

    def x_map(j, table_ref):
        brick = brick_of(j, table_ref)
        return (brick // bricks_z * EDGE, 0, brick % bricks_z * EDGE, 0)

    return pl.pallas_call(
        conv_kernel,
        out_shape=jax.ShapeDtypeStruct((total, C, EDGE**3), jnp.bfloat16),
        grid_spec=pltpu.PrefetchScalarGridSpec(
            num_scalar_prefetch=1,
            grid=(total,),
            in_specs=[
                pl.BlockSpec((pl.Element(EDGE + 2), pl.Element(span), pl.Element(window), pl.Element(depth)), x_map),
                pl.BlockSpec(w9.shape, lambda j, t: (0, 0)),
                pl.BlockSpec(bias_col.shape, lambda j, t: (0, 0)),
                pl.BlockSpec((1, 1, EDGE**3), lambda j, t: (brick_of(j, t), 0, 0)),
            ],
            out_specs=pl.BlockSpec((1, C, EDGE**3), lambda j, t: (j, 0, 0)),
            scratch_shapes=[pltpu.VMEM((3 * C, (EDGE + 2) * EDGE * EDGE), jnp.float32)],
        ),
        compiler_params=pltpu.CompilerParams(vmem_limit_bytes=48 * 1024 * 1024),
    )(table, shifted, w9, bias_col, masks)


def per_device(features, voxel_mask, brick_mask, owner, weights, bias):
    extent_x, extent_y, extent_z, channels_in = features.shape
    bricks_x = extent_x // EDGE
    bricks_y = extent_y // EDGE
    bricks_z = extent_z // EDGE
    count = bricks_x * bricks_y * bricks_z
    groups = lax.axis_size("gy")
    capacity = (count + groups - 1) // groups
    grown = jnp.repeat(brick_mask, EDGE, axis=0)
    grown = jnp.repeat(grown, EDGE, axis=1)
    grown = jnp.repeat(grown, EDGE, axis=2)
    live = (voxel_mask * grown).astype(jnp.bfloat16)
    def masked(index):
        edge = features[index].astype(jnp.float32) * live[index].astype(jnp.float32)[..., None]
        return edge.astype(features.dtype)

    rows_x = lax.axis_size("gx")
    cols_y = lax.axis_size("gy")
    up = lax.ppermute(masked(np.s_[-1:]), "gx", [(i, i + 1) for i in range(rows_x - 1)])
    down = lax.ppermute(masked(np.s_[:1]), "gx", [(i + 1, i) for i in range(rows_x - 1)])
    extended = jnp.concatenate([up, features * live[..., None], down], axis=0)
    col_tail = jnp.concatenate([up[:, -1:], masked(np.s_[:, -1:]), down[:, -1:]], axis=0)
    col_head = jnp.concatenate([up[:, :1], masked(np.s_[:, :1]), down[:, :1]], axis=0)
    left = lax.ppermute(col_tail, "gy", [(i, i + 1) for i in range(cols_y - 1)])
    right = lax.ppermute(col_head, "gy", [(i + 1, i) for i in range(cols_y - 1)])
    padded = jnp.concatenate([left, extended, right], axis=1)
    shifted = jnp.pad(padded, ((0, 0), (0, 0), (1, EDGE - 1), (0, 0)))
    brick_masks = live.astype(jnp.float32).reshape(bricks_x, EDGE, bricks_y, EDGE, bricks_z, EDGE)
    brick_masks = brick_masks.transpose(0, 2, 4, 1, 3, 5).reshape(count, 1, EDGE**3)
    ids = owner.reshape(count)
    order = jnp.arange(count, dtype=jnp.int32)
    same = ids[:, None] == ids[None, :]
    rank = jnp.sum(jnp.logical_and(same, order[None, :] < order[:, None]).astype(jnp.int32), axis=1)
    slots = ids * capacity + rank
    total = groups * capacity
    hit = slots[None, :] == jnp.arange(total, dtype=jnp.int32)[:, None]
    brick_of_slot = jnp.sum(jnp.where(hit, order[None, :], 0), axis=1)
    valid = jnp.any(hit, axis=1).astype(jnp.int32)
    seen = lax.cummax(jnp.where(valid > 0, jnp.arange(total, dtype=jnp.int32), -1))
    first = jnp.argmax(valid)
    held = jnp.where(seen >= 0, brick_of_slot[jnp.maximum(seen, 0)], brick_of_slot[first])
    table = jnp.concatenate([held, valid]).astype(jnp.int32)
    w9 = weights.transpose(1, 2, 3, 0, 4).reshape(9 * channels_in, 3 * C)
    bias_col = bias.reshape(C, 1).astype(jnp.float32)
    sending = conv_slots(table, shifted, w9, bias_col, brick_masks, total, bricks_z)
    decoded = lax.all_to_all(sending, "gy", split_axis=0, concat_axis=0, tiled=True)
    return decoded[None]


def solution(mesh):
    return jax.shard_map(
        per_device,
        mesh=mesh,
        in_specs=(
            P("gx", "gy", None, None),
            P("gx", "gy", None),
            P("gx", "gy", None),
            P("gx", "gy", None, None),
            P(),
            P(),
        ),
        out_specs=P("gx", "gy", None, None),
        check_vma=False,
    )
```
